32 devices in a mesh: groups: 2 (over y), ctx: 16 (over z, x, core).
Axes of the slice: x: 2, y: 2, z: 4, core: 2. Of those that a mesh axis runs over, the one named last changes fastest.
Arguments:
- queries: bfloat16 [8192, 8192], P(('groups', 'ctx')), parts along dimension 0, may hold values from -10 to 10
- keys: bfloat16 [8192, 1024], P(('groups', 'ctx')), parts along dimension 0, may hold values from -6 to 6
- values: bfloat16 [8192, 1024], P(('groups', 'ctx')), parts along dimension 0, may hold values from -6 to 6
- positions: int32 [8192], P(('groups', 'ctx')), parts along dimension 0, may hold values from 0 to 4096, as said below
- picks: int32 [64, 8, 2], P(('groups', 'ctx')), parts along dimension 0, may hold values from -1 to 31, as said below
Outputs:
- attended: bfloat16 [8192, 8192], P(('groups', 'ctx')), parts along dimension 0
The draws below stay inside these ranges and needn't reach their ends.
There are 2 independent parts, one for each index of `groups`. The reference program is written for one: setup_inputs(seed, part) draws one part's arguments, and reference() takes and returns one part's arrays. A program takes and returns all parts, laid end to end along the dimension named above; each array names one. Nothing has to cross between parts.
Inputs may be any that keep to these rules, and one draw needn't show every extreme that they name: positions never fall from one token to the next and each lies in [index, index + 1]; the first is 0 and the last is 4096. A pick of query block b is -1 or a block held by an earlier shard, so its index is below (b // 2) * 2; it may lie inside the band, and then its keys count twice; the two picks of one query block and head differ when both are set, and both are set or both -1; over the 2 query blocks of one shard and all heads, at most 2 picks name blocks of one shard, and some shard has exactly 2 for some other shard in every draw.
All inputs are finite; a program needn't handle non-finite values.
Results may differ from the reference program's by a relative error of at most 0.009.
Values may be sent and summed in bfloat16 or wider, within the bound.
No kernel may reach another device: no remote copies, remote signals or barrier semaphores. Data moves between devices by JAX's collectives and lax.ppermute only.
A program may use at most 192 MiB of HBM per device.

```python
import jax
import jax.numpy as jnp
from jax import lax

QUERY_HEADS = 64
KEY_VALUE_HEADS = 8
HEAD_SIZE = 128
BLOCK_TOKENS = 128
LOCAL_BAND_SIZE = 4
PICKED_BLOCKS = 2
SHARD_BLOCKS = 2
SEQUENCE_BLOCKS = 32
SEQUENCE_TOKENS = 4096
CAP = 2


def draw_keys(key, part):
    rotary_base = jnp.clip(jax.random.normal(jax.random.fold_in(key, 11), (SEQUENCE_TOKENS, KEY_VALUE_HEADS, HEAD_SIZE), jnp.float32), -6.0, 6.0)
    return rotary_base.reshape(SEQUENCE_TOKENS, KEY_VALUE_HEADS * HEAD_SIZE).astype(jnp.bfloat16)


def draw_queries(key, part):
    rotary_base = jnp.clip(jax.random.normal(jax.random.fold_in(key, 12), (SEQUENCE_TOKENS, QUERY_HEADS, HEAD_SIZE), jnp.float32), -6.0, 6.0)
    return rotary_base.reshape(SEQUENCE_TOKENS, QUERY_HEADS * HEAD_SIZE).astype(jnp.bfloat16)


def draw_positions(key, part):
    extra = jax.random.randint(jax.random.fold_in(key, 31), (SEQUENCE_TOKENS,), 0, 2)
    index_value = jnp.arange(SEQUENCE_TOKENS)
    extra = jnp.where(index_value == 0, 0, jnp.where(index_value == SEQUENCE_TOKENS - 1, 1, extra))
    return (index_value + extra).astype(jnp.int32)


def draw_picks(key, part):
    shard_count = SEQUENCE_BLOCKS // SHARD_BLOCKS
    window_length = SHARD_BLOCKS * KEY_VALUE_HEADS
    slots = shard_count * CAP
    needed = 2 * window_length

    def single_shard(shard):
        shard_key = jax.random.fold_in(key, shard)
        last_owner = shard - 1
        is_final = shard == shard_count - 1
        slot_owner = jnp.arange(slots) // CAP
        eligible = slot_owner <= last_owner
        count = jnp.sum(eligible.astype(jnp.int32))
        noise = jax.random.randint(jax.random.fold_in(shard_key, 1), (slots,), 0, 1 << 20)
        score = noise * slots + jnp.arange(slots) + jnp.where(eligible, 0, 1 << 30)
        favored = (slot_owner == last_owner) | is_final & (slot_owner == 0)
        score = jnp.where(favored & eligible, jnp.arange(slots) - slots, score)
        order = jnp.argsort(score).astype(jnp.int32)
        filler = jnp.zeros((max(0, needed - slots),), jnp.int32)
        taken = jnp.concatenate([order, filler])[:needed]
        owners = slot_owner[taken].reshape(window_length, 2)
        live = 2 * jnp.arange(window_length) + 1 < count
        local_first = jax.random.randint(jax.random.fold_in(shard_key, 5), (window_length,), 0, SHARD_BLOCKS)
        local_first = jnp.where(is_final & (owners[:, 0] == 0), SHARD_BLOCKS - 1, local_first)
        stride = jax.random.randint(jax.random.fold_in(shard_key, 6), (window_length,), 1, SHARD_BLOCKS)
        other = jax.random.randint(jax.random.fold_in(shard_key, 7), (window_length,), 0, SHARD_BLOCKS)
        other = jnp.where(is_final & (owners[:, 1] == 0), SHARD_BLOCKS - 1, other)
        local_second = jnp.where(owners[:, 1] == owners[:, 0], (local_first + stride) % SHARD_BLOCKS, other)
        first_choice = jnp.where(live, owners[:, 0] * SHARD_BLOCKS + local_first, -1)
        second_choice = jnp.where(live, owners[:, 1] * SHARD_BLOCKS + local_second, -1)
        return jnp.stack([first_choice, second_choice], -1).reshape(SHARD_BLOCKS, KEY_VALUE_HEADS, 2)
    return jax.vmap(single_shard)(jnp.arange(shard_count)).reshape(SEQUENCE_BLOCKS, KEY_VALUE_HEADS, 2).astype(jnp.int32)


def levels(key, shape, shards, least, top_value):
    loudness = 1.0
    for axis_at, shards_of in shards:
        steps = jax.random.uniform(jax.random.fold_in(jax.random.fold_in(key, 6), axis_at), (shards_of,), jnp.float32, least / len(shards), top_value / len(shards))
        loudness = loudness * jnp.repeat(jnp.exp(steps), shape[axis_at] // shards_of).reshape((-1,) + (1,) * (len(shape) - 1 - axis_at))
    return loudness


def scatter_about(key, dims, spread, most, pieces=(), held_as=jnp.bfloat16):
    values = jax.random.normal(key, dims, jnp.float32) * spread
    if len(pieces) > 0:
        values = levels(key, dims, pieces, -0.22, 0.18) * values
    return jnp.clip(values, min=-most, max=most).astype(held_as)


def setup_inputs(seed: int = 0, part: int = 0) -> dict:
    streams_of = jax.random.split(jax.random.key(seed), 6)
    own_keys = jax.random.split(jax.random.fold_in(streams_of[5], part), 6)
    queries = draw_queries(jax.random.fold_in(jax.random.fold_in(streams_of[5], part), 71), part)
    keys = draw_keys(jax.random.fold_in(jax.random.fold_in(streams_of[5], part), 71), part)
    values = scatter_about(own_keys[2], (SEQUENCE_TOKENS, KEY_VALUE_HEADS * HEAD_SIZE), 1.0, 6.0, ((0, 16),))
    positions = draw_positions(jax.random.fold_in(jax.random.fold_in(streams_of[5], part), 71), part)
    picks = draw_picks(jax.random.fold_in(jax.random.fold_in(streams_of[5], part), 71), part)
    return dict(queries=queries, keys=keys, values=values, positions=positions, picks=picks)


rope_base = 500000.0
masked_score = -1e30


def apply_rotary(x, pos):
    half = x.shape[-1] // 2
    freq = rope_base ** (-(jnp.arange(half, dtype=jnp.float32) * 2.0) / x.shape[-1])
    angle = pos.astype(jnp.float32)[:, None] * freq[None, :]
    cosine = jnp.cos(angle)[:, None, :]
    sine = jnp.sin(angle)[:, None, :]
    wide = x.astype(jnp.float32)
    first_choice = wide[..., :half]
    second_choice = wide[..., half:]
    return jnp.concatenate([first_choice * cosine - second_choice * sine, second_choice * cosine + first_choice * sine], -1).astype(jnp.bfloat16)


def reference(queries, keys, values, positions, picks):
    query_group = QUERY_HEADS // KEY_VALUE_HEADS
    score_scale = HEAD_SIZE ** -0.5
    query_rotated = apply_rotary(queries.reshape(SEQUENCE_TOKENS, QUERY_HEADS, HEAD_SIZE), positions)
    key_rotated = apply_rotary(keys.reshape(SEQUENCE_TOKENS, KEY_VALUE_HEADS, HEAD_SIZE), positions)
    stacked_blocks = jnp.stack([key_rotated, values.reshape(SEQUENCE_TOKENS, KEY_VALUE_HEADS, HEAD_SIZE)], axis=2)
    padded_input = jnp.concatenate([jnp.zeros(((LOCAL_BAND_SIZE - 1) * BLOCK_TOKENS, KEY_VALUE_HEADS, 2, HEAD_SIZE), jnp.bfloat16), stacked_blocks], 0)
    head_numbers = jnp.arange(KEY_VALUE_HEADS, dtype=jnp.int32)
    offsets = jnp.arange(BLOCK_TOKENS, dtype=jnp.int32)

    def one_block(block_number):
        query_block_index = lax.dynamic_slice_in_dim(query_rotated, block_number * BLOCK_TOKENS, BLOCK_TOKENS, 0).reshape(BLOCK_TOKENS, KEY_VALUE_HEADS, query_group, HEAD_SIZE).astype(jnp.float32)
        local_window = lax.dynamic_slice_in_dim(padded_input, block_number * BLOCK_TOKENS, LOCAL_BAND_SIZE * BLOCK_TOKENS, 0).astype(jnp.float32)
        chosen = lax.dynamic_index_in_dim(picks, block_number, 0, keepdims=False)
        start = jnp.maximum(chosen, 0).astype(jnp.int32) * BLOCK_TOKENS
        token_ids = (start[:, :, None] + offsets[None, None, :]).astype(jnp.int32)
        foreign_blocks = stacked_blocks[token_ids, head_numbers[:, None, None]].astype(jnp.float32)
        near_scores = jnp.einsum('qhgd,khd->hgqk', query_block_index, local_window[:, :, 0]) * score_scale
        distant_scores = jnp.einsum('font,ouyt->onfuy', query_block_index, foreign_blocks[:, :, :, 0]).reshape(KEY_VALUE_HEADS, query_group, BLOCK_TOKENS, PICKED_BLOCKS * BLOCK_TOKENS) * score_scale
        key_tok = (block_number - (LOCAL_BAND_SIZE - 1)) * BLOCK_TOKENS + jnp.arange(LOCAL_BAND_SIZE * BLOCK_TOKENS, dtype=jnp.int32)
        query_tok = block_number * BLOCK_TOKENS + offsets
        near_mask = (key_tok[None, :] >= 0) & (key_tok[None, :] <= query_tok[:, None])
        far_mask = jnp.repeat(chosen >= 0, BLOCK_TOKENS, axis=1)[:, None, None, :]
        near_scores = jnp.where(near_mask, near_scores, masked_score)
        distant_scores = jnp.where(far_mask, distant_scores, masked_score)
        top = jnp.maximum(jnp.max(near_scores, -1), jnp.max(distant_scores, -1))[..., None]
        near_exp = jnp.exp(near_scores - top)
        distant_exponent = jnp.exp(distant_scores - top)
        total = jnp.sum(near_exp, -1) + jnp.sum(distant_exponent, -1)
        near_w = lax.optimization_barrier(near_exp.astype(jnp.bfloat16)).astype(jnp.float32)
        distant_weight = lax.optimization_barrier(distant_exponent.astype(jnp.bfloat16)).astype(jnp.float32)
        distant_weight = distant_weight.reshape(KEY_VALUE_HEADS, query_group, BLOCK_TOKENS, PICKED_BLOCKS, BLOCK_TOKENS)
        summed = jnp.einsum('hgqk,khd->qhgd', near_w, local_window[:, :, 1]) + jnp.einsum('hgqpk,hpkd->qhgd', distant_weight, foreign_blocks[:, :, :, 1])
        result = summed / jnp.transpose(total, (2, 0, 1))[..., None]
        return result.reshape(BLOCK_TOKENS, QUERY_HEADS * HEAD_SIZE).astype(jnp.bfloat16)

    blocks = lax.map(one_block, jnp.arange(SEQUENCE_BLOCKS, dtype=jnp.int32))
    return blocks.reshape(SEQUENCE_TOKENS, QUERY_HEADS * HEAD_SIZE)
```

```python
import functools

import jax
import jax.numpy as jnp
from jax import lax
from jax.experimental import pallas as pl
from jax.experimental.pallas import tpu as pltpu
from jax.sharding import PartitionSpec as P

QUERY_HEADS = 64
KEY_VALUE_HEADS = 8
HEAD_SIZE = 128
BLOCK_TOKENS = 128
LOCAL_BAND_SIZE = 4
PICKED_BLOCKS = 2
GROUP = QUERY_HEADS // KEY_VALUE_HEADS
ROWS = GROUP * BLOCK_TOKENS
PAIR = 2 * HEAD_SIZE
BLOCKS = 2

rope_base = 500000.0
masked_score = -1e30
score_factor = HEAD_SIZE ** (-0.5) * 1.4426950408889634

BAND_ROWS = 256
PICK_ROWS = 256

SMEM = pltpu.MemorySpace.SMEM


def from_behind(block, axis, distance):
    devices = range(lax.axis_size(axis))
    route = [(i - distance, i) for i in devices if i - distance in devices]
    return lax.ppermute(block, axis, route)


def rotary_tables(pos):
    half = HEAD_SIZE // 2
    freq = rope_base ** (-(jnp.arange(half, dtype=jnp.float32) * 2.0) / HEAD_SIZE)
    angle = pos.astype(jnp.float32)[:, None] * freq[None, :]
    cosine = jnp.cos(angle)
    sine = jnp.sin(angle)
    return jnp.concatenate([cosine, cosine], -1), jnp.concatenate([-sine, sine], -1)


def rotate(x, cosine, sine):
    wide = x.astype(jnp.float32)
    swapped = pltpu.roll(wide, HEAD_SIZE // 2, 1)
    return (wide * cosine + swapped * sine).astype(jnp.bfloat16)


def prep_kernel(limit, picks_ref, k_ref, v_ref, cos_ref, sin_ref, kv_ref, last_ref, table_ref, slot_ref, count_ref):
    shards = table_ref.shape[0]

    @pl.loop(0, shards)
    def _(i):
        count_ref[i] = 0
        for r in range(limit):
            table_ref[i, r] = -1

    @pl.loop(0, BLOCKS * KEY_VALUE_HEADS)
    def _(i):
        b = i // KEY_VALUE_HEADS
        h = i % KEY_VALUE_HEADS
        for p in range(PICKED_BLOCKS):
            pick = picks_ref[b, h, p]
            slot_ref[i, p] = -1

            @pl.when(pick >= 0)
            def _():
                owner = pick // BLOCKS
                rank = jnp.minimum(count_ref[owner], limit - 1)
                count_ref[owner] = rank + 1
                table_ref[owner, rank] = pick % BLOCKS * KEY_VALUE_HEADS + h
                slot_ref[i, p] = owner * limit + rank

    for b in range(BLOCKS):
        rows = slice(b * BLOCK_TOKENS, (b + 1) * BLOCK_TOKENS)
        cosine = cos_ref[rows, :]
        sine = sin_ref[rows, :]
        for h in range(KEY_VALUE_HEADS):
            cols = slice(h * HEAD_SIZE, (h + 1) * HEAD_SIZE)
            rotated = rotate(k_ref[rows, cols], cosine, sine)
            value = v_ref[rows, cols]
            kv_ref[b, h, :, :HEAD_SIZE] = rotated
            kv_ref[b, h, :, HEAD_SIZE:] = value
            if b == BLOCKS - 1:
                last_ref[0, h, :, :HEAD_SIZE] = rotated
                last_ref[0, h, :, HEAD_SIZE:] = value


def gather_kernel(wanted_ref, kv_ref, out_ref, sems):
    shards, limit = wanted_ref.shape

    def copy(i, r):
        entry = jnp.maximum(wanted_ref[i, r], 0)
        return pltpu.make_async_copy(
            kv_ref.at[entry // KEY_VALUE_HEADS, entry % KEY_VALUE_HEADS],
            out_ref.at[i, r],
            sems.at[i, r],
        )

    @pl.loop(0, shards)
    def _(i):
        for r in range(limit):
            copy(i, r).start()

    @pl.loop(0, shards)
    def _(i):
        for r in range(limit):
            copy(i, r).wait()


def scores_of(query, key):
    return lax.dot_general(query, key, (((1,), (1,)), ((), ())), preferred_element_type=jnp.float32)


def summed(weight, value):
    both = jnp.concatenate([value, jnp.ones_like(value)], 1)
    out = jnp.dot(weight, both, preferred_element_type=jnp.float32)
    return out[:, :HEAD_SIZE], out[:, HEAD_SIZE:]


def band_kernel(me_ref, q_ref, cos_ref, sin_ref, far_ref, near_ref, own_ref, qr_ref, acc_ref, stat_ref):
    me = me_ref[0]
    row = lax.broadcasted_iota(jnp.int32, (BLOCK_TOKENS, BLOCK_TOKENS), 0)
    col = lax.broadcasted_iota(jnp.int32, (BLOCK_TOKENS, BLOCK_TOKENS), 1)
    causal = jnp.concatenate([col <= row] * (BAND_ROWS // BLOCK_TOKENS), 0)
    lane = lax.broadcasted_iota(jnp.int32, (BLOCK_TOKENS, HEAD_SIZE), 1)

    for b in range(BLOCKS):
        rows = slice(b * BLOCK_TOKENS, (b + 1) * BLOCK_TOKENS)
        for g in range(GROUP):
            qr_ref[b, 0, g * BLOCK_TOKENS : (g + 1) * BLOCK_TOKENS, :] = rotate(
                q_ref[rows, g * HEAD_SIZE : (g + 1) * HEAD_SIZE], cos_ref[rows, :], sin_ref[rows, :]
            )

    def attend(start):
        for b in range(BLOCKS):
            pieces = [far_ref[0, 0], near_ref[0, 0], near_ref[1, 0], own_ref[0, 0], own_ref[1, 0]]
            window = jnp.concatenate(pieces[b : b + LOCAL_BAND_SIZE], 0)
            key = window[:, :HEAD_SIZE]
            value = window[:, HEAD_SIZE:]
            stat = jnp.zeros((BLOCK_TOKENS, HEAD_SIZE), jnp.float32)
            for first in range(0, ROWS, BAND_ROWS):
                part = slice(first, first + BAND_ROWS)
                score = scores_of(qr_ref[b, 0, part, :], key)
                edge = (LOCAL_BAND_SIZE - 1) * BLOCK_TOKENS
                before = score[:, :edge]
                if start:
                    oldest = (me * BLOCKS + b - (LOCAL_BAND_SIZE - 1)) * BLOCK_TOKENS
                    index = oldest + lax.broadcasted_iota(jnp.int32, before.shape, 1)
                    before = jnp.where(index >= 0, before, masked_score)
                score = jnp.concatenate([before, jnp.where(causal, score[:, edge:], masked_score)], 1)
                top = jnp.max(score, -1, keepdims=True) * score_factor
                weight = jnp.exp2(score * score_factor - top)
                out, total = summed(weight.astype(jnp.bfloat16), value)
                acc_ref[b, 0, part, :] = out.astype(acc_ref.dtype)
                for g in range(BAND_ROWS // BLOCK_TOKENS):
                    at = slice(g * BLOCK_TOKENS, (g + 1) * BLOCK_TOKENS)
                    head = first // BLOCK_TOKENS + g
                    stat = jnp.where(lane == head, top[at], stat)
                    stat = jnp.where(lane == GROUP + head, total[at], stat)
            stat_ref[b, 0] = stat

    early = me * BLOCKS < LOCAL_BAND_SIZE - 1

    @pl.when(early)
    def _():
        attend(True)

    @pl.when(jnp.logical_not(early))
    def _():
        attend(False)


def picks_kernel(slot_ref, q_ref, first_ref, second_ref, acc_ref, stat_ref, out_ref):
    live = slot_ref[pl.program_id(0), 0] >= 0

    def column(ref_value, at):
        return ref_value[:, at : at + 1]

    @pl.when(live)
    def _():
        window = jnp.concatenate([first_ref[0], second_ref[0]], 0)
        key = window[:, :HEAD_SIZE]
        value = window[:, HEAD_SIZE:]
        stat = stat_ref[0, 0]
        for first in range(0, ROWS, PICK_ROWS):
            part = slice(first, first + PICK_ROWS)
            heads = range(first // BLOCK_TOKENS, (first + PICK_ROWS) // BLOCK_TOKENS)
            score = scores_of(q_ref[0, 0, part, :], key)
            old_top = jnp.concatenate([column(stat, g) for g in heads], 0)
            old_total = jnp.concatenate([column(stat, GROUP + g) for g in heads], 0)
            top = jnp.maximum(jnp.max(score, -1, keepdims=True) * score_factor, old_top)
            weight = jnp.exp2(score * score_factor - top)
            fade = jnp.exp2(old_top - top)
            out, total = summed(weight.astype(jnp.bfloat16), value)
            out = out + acc_ref[0, 0, part, :].astype(jnp.float32) * fade
            result = (out / (total + old_total * fade)).astype(out_ref.dtype)
            for g in heads:
                at = slice(g * BLOCK_TOKENS - first, (g + 1) * BLOCK_TOKENS - first)
                out_ref[:, g * HEAD_SIZE : (g + 1) * HEAD_SIZE] = result[at]

    @pl.when(jnp.logical_not(live))
    def _():
        stat = stat_ref[0, 0]
        for g in range(GROUP):
            acc = acc_ref[0, 0, g * BLOCK_TOKENS : (g + 1) * BLOCK_TOKENS, :].astype(jnp.float32)
            out_ref[:, g * HEAD_SIZE : (g + 1) * HEAD_SIZE] = (acc / column(stat, GROUP + g)).astype(out_ref.dtype)


def shards(queries, keys, values, positions, picks):
    tokens = queries.shape[0]
    window = lax.axis_size("ctx")
    limit = max(1, BLOCKS * KEY_VALUE_HEADS * PICKED_BLOCKS // window)
    me = lax.axis_index("ctx").astype(jnp.int32).reshape(1)
    cosine, sine = rotary_tables(positions)
    bf16 = jnp.bfloat16
    vmem = pl.BlockSpec(memory_space=pltpu.MemorySpace.VMEM)
    smem = pl.BlockSpec(memory_space=SMEM)
    hbm = pl.BlockSpec(memory_space=pl.ANY)

    kv, last, table, slot = pl.pallas_call(
        functools.partial(prep_kernel, limit),
        out_shape=(
            jax.ShapeDtypeStruct((BLOCKS, KEY_VALUE_HEADS, BLOCK_TOKENS, PAIR), bf16),
            jax.ShapeDtypeStruct((1, KEY_VALUE_HEADS, BLOCK_TOKENS, PAIR), bf16),
            jax.ShapeDtypeStruct((window, limit), jnp.int32),
            jax.ShapeDtypeStruct((BLOCKS * KEY_VALUE_HEADS, PICKED_BLOCKS), jnp.int32),
        ),
        in_specs=[smem, vmem, vmem, vmem, vmem],
        out_specs=(vmem, vmem, smem, smem),
        scratch_shapes=[pltpu.SMEM((window,), jnp.int32)],
        name="prep",
    )(picks, keys, values, cosine, sine)

    near = from_behind(kv, "ctx", 1)
    far = from_behind(last, "ctx", 2)
    wanted = lax.all_to_all(table, "ctx", split_axis=0, concat_axis=0, tiled=True)

    answer = pl.pallas_call(
        gather_kernel,
        out_shape=jax.ShapeDtypeStruct((window, limit, BLOCK_TOKENS, PAIR), bf16),
        in_specs=[smem, hbm],
        out_specs=hbm,
        scratch_shapes=[pltpu.SemaphoreType.DMA((window, limit))],
        name="gather",
    )(wanted, kv)
    landed = lax.all_to_all(answer, "ctx", split_axis=0, concat_axis=0, tiled=True)
    landed = landed.reshape(window * limit, BLOCK_TOKENS, PAIR)

    per_head = lambda *shape: pl.BlockSpec((shape[0], 1) + shape[1:], lambda h, *_: (0, h, 0, 0))
    band_flops = 4 * BLOCKS * QUERY_HEADS * BLOCK_TOKENS * LOCAL_BAND_SIZE * BLOCK_TOKENS * HEAD_SIZE
    rotated, acc, stat = pl.pallas_call(
        band_kernel,
        out_shape=(
            jax.ShapeDtypeStruct((BLOCKS, KEY_VALUE_HEADS, ROWS, HEAD_SIZE), bf16),
            jax.ShapeDtypeStruct((BLOCKS, KEY_VALUE_HEADS, ROWS, HEAD_SIZE), bf16),
            jax.ShapeDtypeStruct((BLOCKS, KEY_VALUE_HEADS, BLOCK_TOKENS, HEAD_SIZE), jnp.float32),
        ),
        grid_spec=pltpu.PrefetchScalarGridSpec(
            num_scalar_prefetch=1,
            grid=(KEY_VALUE_HEADS,),
            in_specs=[
                pl.BlockSpec((tokens, ROWS), lambda h, *_: (0, h)),
                pl.BlockSpec((tokens, HEAD_SIZE), lambda h, *_: (0, 0)),
                pl.BlockSpec((tokens, HEAD_SIZE), lambda h, *_: (0, 0)),
                per_head(1, BLOCK_TOKENS, PAIR),
                per_head(BLOCKS, BLOCK_TOKENS, PAIR),
                per_head(BLOCKS, BLOCK_TOKENS, PAIR),
            ],
            out_specs=(
                per_head(BLOCKS, ROWS, HEAD_SIZE),
                per_head(BLOCKS, ROWS, HEAD_SIZE),
                per_head(BLOCKS, BLOCK_TOKENS, HEAD_SIZE),
            ),
        ),
        cost_estimate=pl.CostEstimate(flops=4 * band_flops, bytes_accessed=16 << 20, transcendentals=1 << 23),
        compiler_params=pltpu.CompilerParams(vmem_limit_bytes=32 << 20),
        name="band",
    )(me, queries, cosine, sine, far, near, kv)

    at_slot = lambda p: pl.BlockSpec(
        (1, BLOCK_TOKENS, PAIR), lambda i, slots: (jnp.maximum(slots[i, p], 0), 0, 0)
    )
    per_pair = lambda *shape: pl.BlockSpec(
        (1, 1) + shape, lambda i, *_: (i // KEY_VALUE_HEADS, i % KEY_VALUE_HEADS, 0, 0)
    )
    return pl.pallas_call(
        picks_kernel,
        out_shape=jax.ShapeDtypeStruct((tokens, QUERY_HEADS * HEAD_SIZE), bf16),
        grid_spec=pltpu.PrefetchScalarGridSpec(
            num_scalar_prefetch=1,
            grid=(BLOCKS * KEY_VALUE_HEADS,),
            in_specs=[
                per_pair(ROWS, HEAD_SIZE),
                at_slot(0),
                at_slot(1),
                per_pair(ROWS, HEAD_SIZE),
                per_pair(BLOCK_TOKENS, HEAD_SIZE),
            ],
            out_specs=pl.BlockSpec((BLOCK_TOKENS, ROWS), lambda i, *_: (i // KEY_VALUE_HEADS, i % KEY_VALUE_HEADS)),
        ),
        cost_estimate=pl.CostEstimate(flops=2 * band_flops, bytes_accessed=16 << 20, transcendentals=1 << 22),
        compiler_params=pltpu.CompilerParams(vmem_limit_bytes=32 << 20),
        name="picks",
    )(slot, rotated, landed, landed, acc, stat)


def solution(mesh):
    return jax.shard_map(
        shards,
        mesh=mesh,
        in_specs=(
            P(("groups", "ctx"), None),
            P(("groups", "ctx"), None),
            P(("groups", "ctx"), None),
            P(("groups", "ctx")),
            P(("groups", "ctx"), None, None),
        ),
        out_specs=P(("groups", "ctx"), None),
        check_vma=False,
    )
```

```python
import functools

import jax
import jax.numpy as jnp
from jax import lax
from jax.experimental import pallas as pl
from jax.experimental.pallas import tpu as pltpu
from jax.sharding import PartitionSpec as P

QUERY_HEADS = 64
KEY_VALUE_HEADS = 8
HEAD_SIZE = 128
BLOCK_TOKENS = 128
LOCAL_BAND_SIZE = 4
PICKED_BLOCKS = 2
GROUP = QUERY_HEADS // KEY_VALUE_HEADS
ROWS = GROUP * BLOCK_TOKENS
PAIR = 2 * HEAD_SIZE
BLOCKS = 2

rope_base = 500000.0
masked_score = -1e30
score_factor = HEAD_SIZE ** (-0.5) * 1.4426950408889634

BAND_ROWS = 256
PICK_ROWS = 512
PICK_UNROLL = 4
PICK_AHEAD = 2

SMEM = pltpu.MemorySpace.SMEM


def from_behind(block, axis, distance):
    devices = range(lax.axis_size(axis))
    route = [(i - distance, i) for i in devices if i - distance in devices]
    return lax.ppermute(block, axis, route)


def rotary_tables(pos):
    half = HEAD_SIZE // 2
    freq = rope_base ** (-(jnp.arange(half, dtype=jnp.float32) * 2.0) / HEAD_SIZE)
    angle = pos.astype(jnp.float32)[:, None] * freq[None, :]
    cosine = jnp.cos(angle)
    sine = jnp.sin(angle)
    return jnp.concatenate([cosine, cosine], -1), jnp.concatenate([-sine, sine], -1)


def rotate(x, cosine, sine):
    wide = x.astype(jnp.float32)
    swapped = pltpu.roll(wide, HEAD_SIZE // 2, 1)
    return (wide * cosine + swapped * sine).astype(jnp.bfloat16)


def prep_kernel(limit, picks_ref, k_ref, v_ref, cos_ref, sin_ref, kv_ref, last_ref, table_ref, slot_ref, count_ref):
    shards = table_ref.shape[0]

    @pl.loop(0, shards)
    def _(i):
        count_ref[i] = 0
        for r in range(limit):
            table_ref[i, r] = -1

    @pl.loop(0, BLOCKS * KEY_VALUE_HEADS)
    def _(i):
        b = i // KEY_VALUE_HEADS
        h = i % KEY_VALUE_HEADS
        for p in range(PICKED_BLOCKS):
            pick = picks_ref[b, h, p]
            slot_ref[i, p] = -1

            @pl.when(pick >= 0)
            def _():
                owner = pick // BLOCKS
                rank = jnp.minimum(count_ref[owner], limit - 1)
                count_ref[owner] = rank + 1
                table_ref[owner, rank] = pick % BLOCKS * KEY_VALUE_HEADS + h
                slot_ref[i, p] = owner * limit + rank

    for b in range(BLOCKS):
        rows = slice(b * BLOCK_TOKENS, (b + 1) * BLOCK_TOKENS)
        cosine = cos_ref[rows, :]
        sine = sin_ref[rows, :]
        for h in range(KEY_VALUE_HEADS):
            cols = slice(h * HEAD_SIZE, (h + 1) * HEAD_SIZE)
            rotated = rotate(k_ref[rows, cols], cosine, sine)
            value = v_ref[rows, cols]
            kv_ref[b, h, :, :HEAD_SIZE] = rotated
            kv_ref[b, h, :, HEAD_SIZE:] = value
            if b == BLOCKS - 1:
                last_ref[0, h, :, :HEAD_SIZE] = rotated
                last_ref[0, h, :, HEAD_SIZE:] = value


def gather_kernel(wanted_ref, kv_ref, out_ref, sems):
    shards, limit = wanted_ref.shape

    def copy(i, r):
        entry = jnp.maximum(wanted_ref[i, r], 0)
        return pltpu.make_async_copy(
            kv_ref.at[entry // KEY_VALUE_HEADS, entry % KEY_VALUE_HEADS],
            out_ref.at[i, r],
            sems.at[i, r],
        )

    @pl.loop(0, shards)
    def _(i):
        for r in range(limit):
            copy(i, r).start()

    @pl.loop(0, shards)
    def _(i):
        for r in range(limit):
            copy(i, r).wait()


def scores_of(query, key):
    return lax.dot_general(query, key, (((1,), (1,)), ((), ())), preferred_element_type=jnp.float32)


def summed(weight, value):
    both = jnp.concatenate([value, jnp.ones_like(value)], 1)
    out = jnp.dot(weight, both, preferred_element_type=jnp.float32)
    return out[:, :HEAD_SIZE], out[:, HEAD_SIZE:]


def band_kernel(me_ref, q_ref, cos_ref, sin_ref, far_ref, near_ref, own_ref, qr_ref, acc_ref, lse_ref):
    me = me_ref[0]
    row = lax.broadcasted_iota(jnp.int32, (BLOCK_TOKENS, BLOCK_TOKENS), 0)
    col = lax.broadcasted_iota(jnp.int32, (BLOCK_TOKENS, BLOCK_TOKENS), 1)
    causal = jnp.concatenate([col <= row] * (BAND_ROWS // BLOCK_TOKENS), 0)
    edge = (LOCAL_BAND_SIZE - 1) * BLOCK_TOKENS

    def attend(start, h):
        cols = pl.ds(pl.multiple_of(h * ROWS, ROWS), ROWS)
        pieces = [far_ref[0, h], near_ref[0, h], near_ref[1, h], own_ref[0, h], own_ref[1, h]]
        for b in range(BLOCKS):
            rows = slice(b * BLOCK_TOKENS, (b + 1) * BLOCK_TOKENS)
            query = q_ref[rows, cols]
            cosine = cos_ref[rows, :]
            sine = sin_ref[rows, :]
            window = jnp.concatenate(pieces[b : b + LOCAL_BAND_SIZE], 0)
            key = window[:, :HEAD_SIZE]
            value = window[:, HEAD_SIZE:]
            for first in range(0, ROWS, BAND_ROWS):
                part = slice(first, first + BAND_ROWS)
                rotated = jnp.concatenate(
                    [
                        rotate(query[:, at : at + HEAD_SIZE], cosine, sine)
                        for at in range(first, first + BAND_ROWS, HEAD_SIZE)
                    ],
                    0,
                )
                qr_ref[b, h, part, :] = rotated
                score = scores_of(rotated, key)
                before = score[:, :edge]
                if start:
                    oldest = (me * BLOCKS + b - (LOCAL_BAND_SIZE - 1)) * BLOCK_TOKENS
                    index = oldest + lax.broadcasted_iota(jnp.int32, before.shape, 1)
                    before = jnp.where(index >= 0, before, masked_score)
                score = jnp.concatenate([before, jnp.where(causal, score[:, edge:], masked_score)], 1)
                top = jnp.max(score, -1, keepdims=True) * score_factor
                weight = jnp.exp2(score * score_factor - top)
                out, total = summed(weight.astype(jnp.bfloat16), value)
                acc_ref[b, h, part, :] = (out / total).astype(acc_ref.dtype)
                lse_ref[b, h, part, :] = jnp.log2(total) + top

    early = me * BLOCKS < LOCAL_BAND_SIZE - 1

    @pl.when(early)
    def _():
        pl.loop(0, KEY_VALUE_HEADS)(functools.partial(attend, True))

    @pl.when(jnp.logical_not(early))
    def _():
        pl.loop(0, KEY_VALUE_HEADS)(functools.partial(attend, False))


def picks_kernel(
    slot_ref, q_hbm, landed_hbm, acc_hbm, lse_hbm, out_ref, q_ref, piece_ref, acc_ref, lse_ref, stage_ref, ins, sems
):
    count = BLOCKS * KEY_VALUE_HEADS
    rounds = count // PICK_UNROLL

    def send(i):
        b = i // KEY_VALUE_HEADS
        h = i % KEY_VALUE_HEADS
        return pltpu.make_async_copy(
            stage_ref.at[i],
            out_ref.at[
                pl.ds(pl.multiple_of(b * BLOCK_TOKENS, BLOCK_TOKENS), BLOCK_TOKENS),
                pl.ds(pl.multiple_of(h * ROWS, ROWS), ROWS),
            ],
            sems.at[i],
        )

    def loads(i):
        b = i // KEY_VALUE_HEADS
        h = i % KEY_VALUE_HEADS
        pairs = [
            (landed_hbm.at[jnp.maximum(slot_ref[i, p], 0)], piece_ref.at[i, p]) for p in range(PICKED_BLOCKS)
        ] + [
            (q_hbm.at[b, h], q_ref.at[b, h]),
            (lse_hbm.at[b, h], lse_ref.at[b, h]),
            (acc_hbm.at[b, h], acc_ref.at[b, h]),
        ]
        return [pltpu.make_async_copy(src, dst, ins.at[i, n]) for n, (src, dst) in enumerate(pairs)]

    def start_round(j):
        for u in range(PICK_UNROLL):
            for copy in loads(j * PICK_UNROLL + u):
                copy.start()

    for j in range(min(PICK_AHEAD, rounds)):
        start_round(j)

    @pl.loop(0, rounds)
    def _(j):
        @pl.when(j + PICK_AHEAD < rounds)
        def _():
            start_round(j + PICK_AHEAD)

        for u in range(PICK_UNROLL):
            for copy in loads(j * PICK_UNROLL + u):
                copy.wait()

        for u in range(PICK_UNROLL):
            i = j * PICK_UNROLL + u
            b = i // KEY_VALUE_HEADS
            h = i % KEY_VALUE_HEADS
            bias = jnp.where(slot_ref[i, 0] >= 0, 0.0, masked_score)
            window = piece_ref[i].reshape(PICKED_BLOCKS * BLOCK_TOKENS, PAIR)
            key = window[:, :HEAD_SIZE]
            value = window[:, HEAD_SIZE:]
            for first in range(0, ROWS, PICK_ROWS):
                part = slice(first, first + PICK_ROWS)
                score = scores_of(q_ref[b, h, part, :], key)
                old = lse_ref[b, h, part, :]
                best = jnp.broadcast_to(jnp.max(score, -1, keepdims=True) * score_factor, old.shape) + bias
                top = jnp.maximum(best, old)
                shift = top - bias
                weight = jnp.exp2(score * score_factor - jnp.concatenate([shift] * PICKED_BLOCKS, 1))
                fade = jnp.exp2(old - top)
                out, total = summed(weight.astype(jnp.bfloat16), value)
                out = out + acc_ref[b, h, part, :].astype(jnp.float32) * fade
                result = (out / (total + fade)).astype(stage_ref.dtype)
                for g in range(PICK_ROWS // BLOCK_TOKENS):
                    at = slice(g * BLOCK_TOKENS, (g + 1) * BLOCK_TOKENS)
                    stage_ref[i, :, first + g * HEAD_SIZE : first + (g + 1) * HEAD_SIZE] = result[at]
            send(i).start()

    for i in range(count):
        send(i).wait()


def shards(queries, keys, values, positions, picks):
    tokens = queries.shape[0]
    window = lax.axis_size("ctx")
    limit = max(1, BLOCKS * KEY_VALUE_HEADS * PICKED_BLOCKS // window)
    me = lax.axis_index("ctx").astype(jnp.int32).reshape(1)
    cosine, sine = rotary_tables(positions)
    bf16 = jnp.bfloat16
    vmem = pl.BlockSpec(memory_space=pltpu.MemorySpace.VMEM)
    smem = pl.BlockSpec(memory_space=SMEM)
    hbm = pl.BlockSpec(memory_space=pl.ANY)

    kv, last, table, slot = pl.pallas_call(
        functools.partial(prep_kernel, limit),
        out_shape=(
            jax.ShapeDtypeStruct((BLOCKS, KEY_VALUE_HEADS, BLOCK_TOKENS, PAIR), bf16),
            jax.ShapeDtypeStruct((1, KEY_VALUE_HEADS, BLOCK_TOKENS, PAIR), bf16),
            jax.ShapeDtypeStruct((window, limit), jnp.int32),
            jax.ShapeDtypeStruct((BLOCKS * KEY_VALUE_HEADS, PICKED_BLOCKS), jnp.int32),
        ),
        in_specs=[smem, vmem, vmem, vmem, vmem],
        out_specs=(vmem, vmem, smem, smem),
        scratch_shapes=[pltpu.SMEM((window,), jnp.int32)],
        name="prep",
    )(picks, keys, values, cosine, sine)

    near = from_behind(kv, "ctx", 1)
    far = from_behind(last, "ctx", 2)
    wanted = lax.all_to_all(table, "ctx", split_axis=0, concat_axis=0, tiled=True)

    answer = pl.pallas_call(
        gather_kernel,
        out_shape=jax.ShapeDtypeStruct((window, limit, BLOCK_TOKENS, PAIR), bf16),
        in_specs=[smem, vmem],
        out_specs=hbm,
        scratch_shapes=[pltpu.SemaphoreType.DMA((window, limit))],
        cost_estimate=pl.CostEstimate(flops=0, bytes_accessed=60 << 20, transcendentals=0),
        name="gather",
    )(wanted, kv)
    landed = lax.all_to_all(answer, "ctx", split_axis=0, concat_axis=0, tiled=True)
    landed = landed.reshape(window * limit, BLOCK_TOKENS, PAIR)

    band_flops = 4 * BLOCKS * QUERY_HEADS * BLOCK_TOKENS * LOCAL_BAND_SIZE * BLOCK_TOKENS * HEAD_SIZE
    full = (BLOCKS, KEY_VALUE_HEADS, ROWS, HEAD_SIZE)
    rotated, acc, lse = pl.pallas_call(
        band_kernel,
        out_shape=(
            jax.ShapeDtypeStruct(full, bf16),
            jax.ShapeDtypeStruct(full, bf16),
            jax.ShapeDtypeStruct(full, jnp.float32),
        ),
        in_specs=[smem] + [vmem] * 6,
        out_specs=(vmem,) * 3,
        cost_estimate=pl.CostEstimate(flops=100 * band_flops, bytes_accessed=16 << 20, transcendentals=1 << 23),
        compiler_params=pltpu.CompilerParams(vmem_limit_bytes=30 << 20),
        name="band",
    )(me, queries, cosine, sine, far, near, kv)

    return pl.pallas_call(
        picks_kernel,
        out_shape=jax.ShapeDtypeStruct((tokens, QUERY_HEADS * HEAD_SIZE), bf16),
        in_specs=[smem] + [hbm] * 4,
        out_specs=hbm,
        scratch_shapes=[
            pltpu.VMEM(full, bf16),
            pltpu.VMEM((BLOCKS * KEY_VALUE_HEADS, PICKED_BLOCKS, BLOCK_TOKENS, PAIR), bf16),
            pltpu.VMEM(full, bf16),
            pltpu.VMEM(full, jnp.float32),
            pltpu.VMEM((BLOCKS * KEY_VALUE_HEADS, BLOCK_TOKENS, ROWS), bf16),
            pltpu.SemaphoreType.DMA((BLOCKS * KEY_VALUE_HEADS, PICKED_BLOCKS + 3)),
            pltpu.SemaphoreType.DMA((BLOCKS * KEY_VALUE_HEADS,)),
        ],
        cost_estimate=pl.CostEstimate(flops=2 * band_flops, bytes_accessed=16 << 20, transcendentals=1 << 22),
        compiler_params=pltpu.CompilerParams(vmem_limit_bytes=58 << 20),
        name="picks",
    )(slot, rotated, landed, acc, lse)


def solution(mesh):
    return jax.shard_map(
        shards,
        mesh=mesh,
        in_specs=(
            P(("groups", "ctx"), None),
            P(("groups", "ctx"), None),
            P(("groups", "ctx"), None),
            P(("groups", "ctx")),
            P(("groups", "ctx"), None, None),
        ),
        out_specs=P(("groups", "ctx"), None),
        check_vma=False,
    )
```

```python
import functools

import jax
import jax.numpy as jnp
from jax import lax
from jax.experimental import pallas as pl
from jax.experimental.pallas import tpu as pltpu
from jax.sharding import PartitionSpec as P

QUERY_HEADS = 64
KEY_VALUE_HEADS = 8
HEAD_SIZE = 128
BLOCK_TOKENS = 128
LOCAL_BAND_SIZE = 4
PICKED_BLOCKS = 2
KEY_WIDTH = KEY_VALUE_HEADS * HEAD_SIZE
GROUP = QUERY_HEADS // KEY_VALUE_HEADS
ROWS = GROUP * BLOCK_TOKENS
PAIR = 2 * HEAD_SIZE
BLOCKS = 2

rope_base = 500000.0
masked_score = -1e30
score_factor = HEAD_SIZE ** (-0.5) * 1.4426950408889634

BAND_ROWS = 256
PICK_ROWS = 512
PICK_UNROLL = 2
PICK_AHEAD = 2

SMEM = pltpu.MemorySpace.SMEM


def rotary_tables(pos):
    half = HEAD_SIZE // 2
    freq = rope_base ** (-(jnp.arange(half, dtype=jnp.float32) * 2.0) / HEAD_SIZE)
    angle = pos.astype(jnp.float32)[:, None] * jnp.concatenate([freq, freq])[None, :]
    sign = jnp.where(jnp.arange(HEAD_SIZE) < half, -1.0, 1.0)
    return jnp.cos(angle), jnp.sin(angle) * sign[None, :]


def rotate(x, cosine, sine):
    wide = x.astype(jnp.float32)
    swapped = pltpu.roll(wide, HEAD_SIZE // 2, 1)
    return (wide * cosine + swapped * sine).astype(jnp.bfloat16)


def prep_kernel(limit, picks_ref, k_ref, v_ref, cos_ref, sin_ref, kr_ref, last_ref, table_ref, slot_ref, count_ref):
    shards = table_ref.shape[0]

    @pl.loop(0, shards)
    def _(i):
        count_ref[i] = 0
        for r in range(limit):
            table_ref[i, 0, r] = -1

    @pl.loop(0, BLOCKS * KEY_VALUE_HEADS)
    def _(i):
        b = i // KEY_VALUE_HEADS
        h = i % KEY_VALUE_HEADS
        for p in range(PICKED_BLOCKS):
            pick = picks_ref[b, p, h]
            slot_ref[i, p] = -1

            @pl.when(pick >= 0)
            def _():
                owner = pick // BLOCKS
                rank = jnp.minimum(count_ref[owner], limit - 1)
                count_ref[owner] = rank + 1
                table_ref[owner, 0, rank] = pick % BLOCKS * KEY_VALUE_HEADS + h
                slot_ref[i, p] = owner * limit + rank

    for b in range(BLOCKS):
        rows = slice(b * BLOCK_TOKENS, (b + 1) * BLOCK_TOKENS)
        cosine = cos_ref[rows, :]
        sine = sin_ref[rows, :]
        for h in range(KEY_VALUE_HEADS):
            cols = slice(h * HEAD_SIZE, (h + 1) * HEAD_SIZE)
            rotated = rotate(k_ref[rows, cols], cosine, sine)
            kr_ref[rows, cols] = rotated
            if b == BLOCKS - 1:
                last_ref[:, cols] = rotated
    last_ref[:, KEY_WIDTH:] = v_ref[(BLOCKS - 1) * BLOCK_TOKENS :, :]


def gather_kernel(wanted_ref, k_ref, v_ref, out_ref, sems):
    shards, _, limit = wanted_ref.shape

    def copies(i, r):
        entry = jnp.maximum(wanted_ref[i, 0, r], 0)
        rows = pl.ds(pl.multiple_of(entry // KEY_VALUE_HEADS * BLOCK_TOKENS, BLOCK_TOKENS), BLOCK_TOKENS)
        cols = pl.ds(pl.multiple_of(entry % KEY_VALUE_HEADS * HEAD_SIZE, HEAD_SIZE), HEAD_SIZE)
        return [
            pltpu.make_async_copy(src.at[rows, cols], out_ref.at[i, r, n], sems.at[n, i, r])
            for n, src in enumerate((k_ref, v_ref))
        ]

    @pl.loop(0, shards)
    def _(i):
        for r in range(limit):
            for copy in copies(i, r):
                copy.start()

    @pl.loop(0, shards)
    def _(i):
        for r in range(limit):
            for copy in copies(i, r):
                copy.wait()


def scores_of(query, key):
    return lax.dot_general(query, key, (((1,), (1,)), ((), ())), preferred_element_type=jnp.float32)


def summed(weight, value):
    both = jnp.concatenate([value, jnp.ones_like(value)], 1)
    out = jnp.dot(weight, both, preferred_element_type=jnp.float32)
    return out[:, :HEAD_SIZE], out[:, HEAD_SIZE:]


def band_kernel(b, me_ref, q_ref, cos_ref, sin_ref, nk_ref, nv_ref, k_ref, v_ref, *rest):
    far_refs = rest[:-3]
    qr_ref, acc_ref, lse_ref = rest[-3:]
    me = me_ref[0]
    row = lax.broadcasted_iota(jnp.int32, (BLOCK_TOKENS, BLOCK_TOKENS), 0)
    col = lax.broadcasted_iota(jnp.int32, (BLOCK_TOKENS, BLOCK_TOKENS), 1)
    causal = jnp.concatenate([col <= row] * (BAND_ROWS // BLOCK_TOKENS), 0)
    edge = (LOCAL_BAND_SIZE - 1) * BLOCK_TOKENS
    own = (b + 1) * BLOCK_TOKENS
    rows = slice(b * BLOCK_TOKENS, (b + 1) * BLOCK_TOKENS)

    def attend(start, h):
        at_key = pl.ds(pl.multiple_of(h * HEAD_SIZE, HEAD_SIZE), HEAD_SIZE)
        at_value = pl.ds(pl.multiple_of(KEY_WIDTH + h * HEAD_SIZE, HEAD_SIZE), HEAD_SIZE)
        keys = [nk_ref[:, at_key], k_ref[:own, at_key]]
        values = [nv_ref[:, at_key], v_ref[:own, at_key]]
        if far_refs:
            even_ref, odd_ref = far_refs
            odd = me % 2 == 1
            keys = [jnp.where(odd, odd_ref[:, at_key], even_ref[:, at_key])] + keys
            values = [jnp.where(odd, odd_ref[:, at_value], even_ref[:, at_value])] + values
        key = jnp.concatenate(keys, 0)
        value = jnp.concatenate(values, 0)
        query = q_ref[rows, pl.ds(pl.multiple_of(h * ROWS, ROWS), ROWS)]
        for first in range(0, ROWS, BAND_ROWS):
            part = slice(first, first + BAND_ROWS)
            rotated = jnp.concatenate(
                [
                    rotate(query[:, at : at + HEAD_SIZE], cos_ref[rows, :], sin_ref[rows, :])
                    for at in range(first, first + BAND_ROWS, HEAD_SIZE)
                ],
                0,
            )
            qr_ref[h, part, :] = rotated
            score = scores_of(rotated, key)
            before = score[:, :edge]
            if start:
                oldest = (me * BLOCKS + b - (LOCAL_BAND_SIZE - 1)) * BLOCK_TOKENS
                index = oldest + lax.broadcasted_iota(jnp.int32, before.shape, 1)
                before = jnp.where(index >= 0, before, masked_score)
            score = jnp.concatenate([before, jnp.where(causal, score[:, edge:], masked_score)], 1)
            top = jnp.max(score, -1, keepdims=True) * score_factor
            weight = jnp.exp2(score * score_factor - top)
            out, total = summed(weight.astype(jnp.bfloat16), value)
            acc_ref[h, part, :] = (out / total).astype(acc_ref.dtype)
            lse_ref[h, part, :] = jnp.log2(total) + top

    early = me * BLOCKS + b < LOCAL_BAND_SIZE - 1

    @pl.when(early)
    def _():
        pl.loop(0, KEY_VALUE_HEADS)(functools.partial(attend, True))

    @pl.when(jnp.logical_not(early))
    def _():
        pl.loop(0, KEY_VALUE_HEADS)(functools.partial(attend, False))


def picks_kernel(slot_ref, landed_hbm, *rest):
    band_hbm = rest[: 3 * BLOCKS]
    out_hbm, q_ref, piece_ref, acc_ref, lse_ref, out_ref, ins, outs = rest[3 * BLOCKS :]
    rounds = KEY_VALUE_HEADS // PICK_UNROLL

    def loads(b, h):
        i = b * KEY_VALUE_HEADS + h
        pairs = [(landed_hbm.at[jnp.maximum(slot_ref[i, p], 0)], piece_ref.at[i, p]) for p in range(PICKED_BLOCKS)]
        pairs += [(src.at[h], dst.at[i]) for src, dst in zip(band_hbm[3 * b : 3 * b + 3], (q_ref, acc_ref, lse_ref))]
        return [pltpu.make_async_copy(src, dst, ins.at[i, n]) for n, (src, dst) in enumerate(pairs)]

    def store(b, h):
        i = b * KEY_VALUE_HEADS + h
        rows = pl.ds(b * BLOCK_TOKENS, BLOCK_TOKENS)
        cols = pl.ds(pl.multiple_of(h * ROWS, ROWS), ROWS)
        return pltpu.make_async_copy(out_ref.at[i], out_hbm.at[rows, cols], outs.at[i])

    def start_round(b, j):
        for u in range(PICK_UNROLL):
            for copy in loads(b, j * PICK_UNROLL + u):
                copy.start()

    def step(i):
        bias = jnp.where(slot_ref[i, 0] >= 0, 0.0, masked_score)
        key = jnp.concatenate([piece_ref[i, p, 0] for p in range(PICKED_BLOCKS)], 0)
        value = jnp.concatenate([piece_ref[i, p, 1] for p in range(PICKED_BLOCKS)], 0)
        for first in range(0, ROWS, PICK_ROWS):
            part = slice(first, first + PICK_ROWS)
            score = scores_of(q_ref[i, part, :], key)
            old = lse_ref[i, part, :]
            best = jnp.broadcast_to(jnp.max(score, -1, keepdims=True) * score_factor, old.shape) + bias
            top = jnp.maximum(best, old)
            shift = top - bias
            weight = jnp.exp2(score * score_factor - jnp.concatenate([shift] * PICKED_BLOCKS, 1))
            fade = jnp.exp2(old - top)
            out, total = summed(weight.astype(jnp.bfloat16), value)
            out = out + acc_ref[i, part, :].astype(jnp.float32) * fade
            result = (out / (total + fade)).astype(out_ref.dtype)
            for g in range(PICK_ROWS // BLOCK_TOKENS):
                at = slice(g * BLOCK_TOKENS, (g + 1) * BLOCK_TOKENS)
                out_ref[i, :, first + g * HEAD_SIZE : first + (g + 1) * HEAD_SIZE] = result[at]

    for j in range(PICK_AHEAD):
        start_round(0, j)

    for b in range(BLOCKS):

        @pl.loop(0, rounds)
        def _(j):
            @pl.when(j + PICK_AHEAD < rounds)
            def _():
                start_round(b, j + PICK_AHEAD)

            if b + 1 < BLOCKS:

                @pl.when(j + PICK_AHEAD >= rounds)
                def _():
                    start_round(b + 1, j + PICK_AHEAD - rounds)

            for u in range(PICK_UNROLL):
                for copy in loads(b, j * PICK_UNROLL + u):
                    copy.wait()

            for u in range(PICK_UNROLL):
                h = j * PICK_UNROLL + u
                step(b * KEY_VALUE_HEADS + h)
                store(b, h).start()

    for b in range(BLOCKS):
        for h in range(KEY_VALUE_HEADS):
            store(b, h).wait()


def shards(queries, keys, values, positions, picks):
    tokens = queries.shape[0]
    window = lax.axis_size("ctx")
    limit = max(1, BLOCKS * KEY_VALUE_HEADS * PICKED_BLOCKS // window)
    me = lax.axis_index("ctx").astype(jnp.int32).reshape(1)
    cosine, sine = rotary_tables(positions)
    bf16 = jnp.bfloat16
    vmem = pl.BlockSpec(memory_space=pltpu.MemorySpace.VMEM)
    smem = pl.BlockSpec(memory_space=SMEM)
    hbm = pl.BlockSpec(memory_space=pl.ANY)

    near_v = lax.ppermute(values, "ctx", [(i - 1, i) for i in range(1, window)])
    rotated_keys, last, table, slot = pl.pallas_call(
        functools.partial(prep_kernel, limit),
        out_shape=(
            jax.ShapeDtypeStruct((tokens, KEY_WIDTH), bf16),
            jax.ShapeDtypeStruct((BLOCK_TOKENS, 2 * KEY_WIDTH), bf16),
            jax.ShapeDtypeStruct((window, 1, limit), jnp.int32),
            jax.ShapeDtypeStruct((BLOCKS * KEY_VALUE_HEADS, PICKED_BLOCKS), jnp.int32),
        ),
        in_specs=[smem, vmem, vmem, vmem, vmem],
        out_specs=(vmem, vmem, smem, smem),
        scratch_shapes=[pltpu.SMEM((window,), jnp.int32)],
        name="prep",
    )(picks.transpose(0, 2, 1), keys, values, cosine, sine)

    near_k = lax.ppermute(rotated_keys, "ctx", [(i - 1, i) for i in range(1, window)])
    wanted = lax.all_to_all(table, "ctx", split_axis=0, concat_axis=0, tiled=True)
    wanted, last, near_k, near_v = lax.optimization_barrier((wanted, last, near_k, near_v))
    far_even = lax.ppermute(last, "ctx", [(i - 2, i) for i in range(2, window, 2)])

    answer = pl.pallas_call(
        gather_kernel,
        out_shape=jax.ShapeDtypeStruct((window, limit, 2, BLOCK_TOKENS, HEAD_SIZE), bf16),
        in_specs=[smem, vmem, vmem],
        out_specs=hbm,
        scratch_shapes=[pltpu.SemaphoreType.DMA((2, window, limit))],
        cost_estimate=pl.CostEstimate(flops=0, bytes_accessed=60 << 20, transcendentals=0),
        name="gather",
    )(wanted, rotated_keys, values)
    landed = lax.all_to_all(answer, "ctx", split_axis=0, concat_axis=0, tiled=True)
    landed = landed.reshape(window * limit, 2, BLOCK_TOKENS, HEAD_SIZE)

    band_flops = 4 * BLOCKS * QUERY_HEADS * BLOCK_TOKENS * LOCAL_BAND_SIZE * BLOCK_TOKENS * HEAD_SIZE
    full = (KEY_VALUE_HEADS, ROWS, HEAD_SIZE)

    def band(b, weight, *far):
        return pl.pallas_call(
            functools.partial(band_kernel, b),
            out_shape=(
                jax.ShapeDtypeStruct(full, bf16),
                jax.ShapeDtypeStruct(full, bf16),
                jax.ShapeDtypeStruct(full, jnp.float32),
            ),
            in_specs=[smem] + [vmem] * (7 + len(far)),
            out_specs=(vmem,) * 3,
            cost_estimate=pl.CostEstimate(flops=weight * band_flops, bytes_accessed=8 << 20, transcendentals=1 << 22),
            compiler_params=pltpu.CompilerParams(vmem_limit_bytes=30 << 20),
            name="band",
        )(me, queries, cosine, sine, near_k, near_v, rotated_keys, values, *far)

    second = band(1, 50)
    edge_k, edge_v, _ = lax.optimization_barrier((near_k, near_v, second[2]))
    edge = jnp.concatenate([edge_k[tokens - BLOCK_TOKENS :], edge_v[tokens - BLOCK_TOKENS :]], 1)
    far_odd = lax.ppermute(edge, "ctx", [(i - 1, i) for i in range(1, window, 2)])
    first = band(0, 1, far_even, far_odd)

    count = BLOCKS * KEY_VALUE_HEADS
    narrow = (count, ROWS, HEAD_SIZE)
    return pl.pallas_call(
        picks_kernel,
        out_shape=jax.ShapeDtypeStruct((tokens, QUERY_HEADS * HEAD_SIZE), bf16),
        in_specs=[smem] + [hbm] * (1 + 3 * BLOCKS),
        out_specs=hbm,
        scratch_shapes=[
            pltpu.VMEM(narrow, bf16),
            pltpu.VMEM((count, PICKED_BLOCKS, 2, BLOCK_TOKENS, HEAD_SIZE), bf16),
            pltpu.VMEM(narrow, bf16),
            pltpu.VMEM(narrow, jnp.float32),
            pltpu.VMEM((count, BLOCK_TOKENS, ROWS), bf16),
            pltpu.SemaphoreType.DMA((count, PICKED_BLOCKS + 3)),
            pltpu.SemaphoreType.DMA((count,)),
        ],
        cost_estimate=pl.CostEstimate(flops=2 * band_flops, bytes_accessed=16 << 20, transcendentals=1 << 22),
        compiler_params=pltpu.CompilerParams(vmem_limit_bytes=58 << 20),
        name="picks",
    )(slot, landed, *first, *second)


def solution(mesh):
    return jax.shard_map(
        shards,
        mesh=mesh,
        in_specs=(
            P(("groups", "ctx"), None),
            P(("groups", "ctx"), None),
            P(("groups", "ctx"), None),
            P(("groups", "ctx")),
            P(("groups", "ctx"), None, None),
        ),
        out_specs=P(("groups", "ctx"), None),
        check_vma=False,
    )
```

```python
import functools

import jax
import jax.numpy as jnp
from jax import lax
from jax.experimental import pallas as pl
from jax.experimental.pallas import tpu as pltpu
from jax.sharding import PartitionSpec as P

QUERY_HEADS = 64
KEY_VALUE_HEADS = 8
HEAD_SIZE = 128
BLOCK_TOKENS = 128
LOCAL_BAND_SIZE = 4
PICKED_BLOCKS = 2
KEY_WIDTH = KEY_VALUE_HEADS * HEAD_SIZE
GROUP = QUERY_HEADS // KEY_VALUE_HEADS
ROWS = GROUP * BLOCK_TOKENS
PAIR = 2 * HEAD_SIZE
BLOCKS = 2

rope_base = 500000.0
masked_score = -1e30
score_factor = HEAD_SIZE ** (-0.5) * 1.4426950408889634

PARTS = 3

BAND_ROWS = 256
PICK_ROWS = 512
PICK_UNROLL = 4
PICK_AHEAD = 2

SMEM = pltpu.MemorySpace.SMEM


def rotary_tables(pos):
    half = HEAD_SIZE // 2
    freq = rope_base ** (-(jnp.arange(half, dtype=jnp.float32) * 2.0) / HEAD_SIZE)
    angle = pos.astype(jnp.float32)[:, None] * jnp.concatenate([freq, freq])[None, :]
    sign = jnp.where(jnp.arange(HEAD_SIZE) < half, -1.0, 1.0)
    return jnp.cos(angle), jnp.sin(angle) * sign[None, :]


def rotate(x, cosine, sine):
    wide = x.astype(jnp.float32)
    swapped = pltpu.roll(wide, HEAD_SIZE // 2, 1)
    return (wide * cosine + swapped * sine).astype(jnp.bfloat16)


def prep_kernel(limit, picks_ref, k_ref, v_ref, cos_ref, sin_ref, kr_ref, last_ref, table_ref, slot_ref, count_ref):
    shards = table_ref.shape[0]

    @pl.loop(0, shards)
    def _(i):
        count_ref[i] = 0
        for r in range(limit):
            table_ref[i, 0, r] = -1

    @pl.loop(0, BLOCKS * KEY_VALUE_HEADS)
    def _(i):
        b = i // KEY_VALUE_HEADS
        h = i % KEY_VALUE_HEADS
        for p in range(PICKED_BLOCKS):
            pick = picks_ref[b, p, h]
            slot_ref[i, p] = -1

            @pl.when(pick >= 0)
            def _():
                owner = pick // BLOCKS
                rank = jnp.minimum(count_ref[owner], limit - 1)
                count_ref[owner] = rank + 1
                table_ref[owner, 0, rank] = pick % BLOCKS * KEY_VALUE_HEADS + h
                slot_ref[i, p] = owner * limit + rank

    for b in range(BLOCKS):
        rows = slice(b * BLOCK_TOKENS, (b + 1) * BLOCK_TOKENS)
        cosine = cos_ref[rows, :]
        sine = sin_ref[rows, :]
        for h in range(KEY_VALUE_HEADS):
            cols = slice(h * HEAD_SIZE, (h + 1) * HEAD_SIZE)
            rotated = rotate(k_ref[rows, cols], cosine, sine)
            kr_ref[rows, cols] = rotated
            if b == BLOCKS - 1:
                last_ref[:, cols] = rotated
    last_ref[:, KEY_WIDTH:] = v_ref[(BLOCKS - 1) * BLOCK_TOKENS :, :]


def gather_kernel(wanted_ref, k_ref, v_ref, out_ref, sems):
    shards, _, limit = wanted_ref.shape

    def copies(i, r):
        entry = jnp.maximum(wanted_ref[i, 0, r], 0)
        rows = pl.ds(pl.multiple_of(entry // KEY_VALUE_HEADS * BLOCK_TOKENS, BLOCK_TOKENS), BLOCK_TOKENS)
        cols = pl.ds(pl.multiple_of(entry % KEY_VALUE_HEADS * HEAD_SIZE, HEAD_SIZE), HEAD_SIZE)
        return [
            pltpu.make_async_copy(src.at[rows, cols], out_ref.at[i, r, n], sems.at[n, i, r])
            for n, src in enumerate((k_ref, v_ref))
        ]

    @pl.loop(0, shards)
    def _(i):
        for r in range(limit):
            for copy in copies(i, r):
                copy.start()

    @pl.loop(0, shards)
    def _(i):
        for r in range(limit):
            for copy in copies(i, r):
                copy.wait()


def scores_of(query, key):
    return lax.dot_general(query, key, (((1,), (1,)), ((), ())), preferred_element_type=jnp.float32)


def summed(weight, value):
    both = jnp.concatenate([value, jnp.ones_like(value)], 1)
    out = jnp.dot(weight, both, preferred_element_type=jnp.float32)
    return out[:, :HEAD_SIZE], out[:, HEAD_SIZE:]


def band_kernel(b, me_ref, q_ref, cos_ref, sin_ref, nk_ref, nv_ref, k_ref, v_ref, *rest):
    far_refs = rest[:-3]
    qr_ref, acc_ref, sums_ref = rest[-3:]
    lane = lax.broadcasted_iota(jnp.int32, (BAND_ROWS, HEAD_SIZE), 1)
    sums_ref[...] = jnp.zeros_like(sums_ref)
    me = me_ref[0]
    row = lax.broadcasted_iota(jnp.int32, (BLOCK_TOKENS, BLOCK_TOKENS), 0)
    col = lax.broadcasted_iota(jnp.int32, (BLOCK_TOKENS, BLOCK_TOKENS), 1)
    causal = jnp.concatenate([col <= row] * (BAND_ROWS // BLOCK_TOKENS), 0)
    edge = (LOCAL_BAND_SIZE - 1) * BLOCK_TOKENS
    own = (b + 1) * BLOCK_TOKENS
    rows = slice(b * BLOCK_TOKENS, (b + 1) * BLOCK_TOKENS)

    def attend(start, h):
        at_key = pl.ds(pl.multiple_of(h * HEAD_SIZE, HEAD_SIZE), HEAD_SIZE)
        at_value = pl.ds(pl.multiple_of(KEY_WIDTH + h * HEAD_SIZE, HEAD_SIZE), HEAD_SIZE)
        keys = [nk_ref[:, at_key], k_ref[:own, at_key]]
        values = [nv_ref[:, at_key], v_ref[:own, at_key]]
        if far_refs:
            even_ref, odd_ref = far_refs
            odd = me % 2 == 1
            keys = [jnp.where(odd, odd_ref[:, at_key], even_ref[:, at_key])] + keys
            values = [jnp.where(odd, odd_ref[:, at_value], even_ref[:, at_value])] + values
        key = jnp.concatenate(keys, 0)
        value = jnp.concatenate(values, 0)
        query = q_ref[rows, pl.ds(pl.multiple_of(h * ROWS, ROWS), ROWS)]
        for first in range(0, ROWS, BAND_ROWS):
            part = slice(first, first + BAND_ROWS)
            rotated = jnp.concatenate(
                [
                    rotate(query[:, at : at + HEAD_SIZE], cos_ref[rows, :], sin_ref[rows, :])
                    for at in range(first, first + BAND_ROWS, HEAD_SIZE)
                ],
                0,
            )
            qr_ref[h, part, :] = rotated
            score = scores_of(rotated, key)
            before = score[:, :edge]
            if start:
                oldest = (me * BLOCKS + b - (LOCAL_BAND_SIZE - 1)) * BLOCK_TOKENS
                index = oldest + lax.broadcasted_iota(jnp.int32, before.shape, 1)
                before = jnp.where(index >= 0, before, masked_score)
            score = jnp.concatenate([before, jnp.where(causal, score[:, edge:], masked_score)], 1)
            top = jnp.max(score, -1, keepdims=True) * score_factor
            weight = jnp.exp2(score * score_factor - top)
            out, total = summed(weight.astype(jnp.bfloat16), value)
            acc_ref[h, part, :] = (out / total).astype(acc_ref.dtype)
            left = (jnp.log2(total) + top) * (1.0 / score_factor)
            sums = sums_ref[part, :].astype(jnp.float32)
            for n in range(PARTS):
                addend = left.astype(jnp.bfloat16).astype(jnp.float32)
                sums = jnp.where(lane == PARTS * h + n, addend, sums)
                left = left - addend
            sums_ref[part, :] = sums.astype(sums_ref.dtype)

    early = me * BLOCKS + b < LOCAL_BAND_SIZE - 1

    @pl.when(early)
    def _():
        pl.loop(0, KEY_VALUE_HEADS)(functools.partial(attend, True))

    @pl.when(jnp.logical_not(early))
    def _():
        pl.loop(0, KEY_VALUE_HEADS)(functools.partial(attend, False))


def picks_kernel(slot_ref, landed_hbm, *rest):
    band_hbm = rest[: 3 * BLOCKS]
    out_hbm, q_ref, piece_ref, acc_ref, sums_ref, out_ref, ins, outs, sums_sems = rest[3 * BLOCKS :]
    rounds = KEY_VALUE_HEADS // PICK_UNROLL

    def loads(b, h):
        i = b * KEY_VALUE_HEADS + h
        pairs = [(landed_hbm.at[jnp.maximum(slot_ref[i, p], 0)], piece_ref.at[i, p]) for p in range(PICKED_BLOCKS)]
        pairs += [(src.at[h], dst.at[i]) for src, dst in zip(band_hbm[3 * b : 3 * b + 2], (q_ref, acc_ref))]
        return [pltpu.make_async_copy(src, dst, ins.at[i, n]) for n, (src, dst) in enumerate(pairs)]

    def store(b, h):
        i = b * KEY_VALUE_HEADS + h
        rows = pl.ds(b * BLOCK_TOKENS, BLOCK_TOKENS)
        cols = pl.ds(pl.multiple_of(h * ROWS, ROWS), ROWS)
        return pltpu.make_async_copy(out_ref.at[i], out_hbm.at[rows, cols], outs.at[i])

    def start_round(b, j):
        for u in range(PICK_UNROLL):
            for copy in loads(b, j * PICK_UNROLL + u):
                copy.start()

    def sums_load(b):
        return pltpu.make_async_copy(band_hbm[3 * b + 2], sums_ref.at[b], sums_sems.at[b])

    def step(b, h):
        i = b * KEY_VALUE_HEADS + h
        bias = jnp.where(slot_ref[i, 0] >= 0, 0.0, masked_score)
        key = jnp.concatenate([piece_ref[i, p, 0] for p in range(PICKED_BLOCKS)], 0)
        lane = lax.broadcasted_iota(jnp.int32, key.shape, 1)
        minus = jnp.where((lane >= PARTS * h) & (lane < PARTS * h + PARTS), -1.0, 0.0).astype(key.dtype)
        key = jnp.concatenate([key, minus], 1)
        value = jnp.concatenate([piece_ref[i, p, 1] for p in range(PICKED_BLOCKS)], 0)
        for first in range(0, ROWS, PICK_ROWS):
            part = slice(first, first + PICK_ROWS)
            score = scores_of(jnp.concatenate([q_ref[i, part, :], sums_ref[b, part, :]], 1), key)
            best = jnp.max(score, -1, keepdims=True) * score_factor + bias
            top = jnp.maximum(jnp.broadcast_to(best, (PICK_ROWS, HEAD_SIZE)), 0.0)
            shift = top - bias
            weight = jnp.exp2(score * score_factor - jnp.concatenate([shift] * PICKED_BLOCKS, 1))
            fade = jnp.exp2(-top)
            out, total = summed(weight.astype(jnp.bfloat16), value)
            out = out + acc_ref[i, part, :].astype(jnp.float32) * fade
            result = (out / (total + fade)).astype(out_ref.dtype)
            for g in range(PICK_ROWS // BLOCK_TOKENS):
                at = slice(g * BLOCK_TOKENS, (g + 1) * BLOCK_TOKENS)
                out_ref[i, :, first + g * HEAD_SIZE : first + (g + 1) * HEAD_SIZE] = result[at]

    sums_load(0).start()
    for j in range(PICK_AHEAD):
        start_round(0, j)
    for b in range(1, BLOCKS):
        sums_load(b).start()

    for b in range(BLOCKS):
        sums_load(b).wait()

        @pl.loop(0, rounds)
        def _(j):
            @pl.when(j + PICK_AHEAD < rounds)
            def _():
                start_round(b, j + PICK_AHEAD)

            if b + 1 < BLOCKS:

                @pl.when(j + PICK_AHEAD >= rounds)
                def _():
                    start_round(b + 1, j + PICK_AHEAD - rounds)

            for u in range(PICK_UNROLL):
                for copy in loads(b, j * PICK_UNROLL + u):
                    copy.wait()

            for u in range(PICK_UNROLL):
                h = j * PICK_UNROLL + u
                step(b, h)
                store(b, h).start()

    for b in range(BLOCKS):
        for h in range(KEY_VALUE_HEADS):
            store(b, h).wait()


def shards(queries, keys, values, positions, picks):
    tokens = queries.shape[0]
    window = lax.axis_size("ctx")
    limit = max(1, BLOCKS * KEY_VALUE_HEADS * PICKED_BLOCKS // window)
    me = lax.axis_index("ctx").astype(jnp.int32).reshape(1)
    cosine, sine = rotary_tables(positions)
    bf16 = jnp.bfloat16
    vmem = pl.BlockSpec(memory_space=pltpu.MemorySpace.VMEM)
    smem = pl.BlockSpec(memory_space=SMEM)
    hbm = pl.BlockSpec(memory_space=pl.ANY)

    behind = [((i - 1) % window, i) for i in range(window)]
    near_v = lax.ppermute(values, "ctx", behind)
    rotated_keys, last, table, slot = pl.pallas_call(
        functools.partial(prep_kernel, limit),
        out_shape=(
            jax.ShapeDtypeStruct((tokens, KEY_WIDTH), bf16),
            jax.ShapeDtypeStruct((BLOCK_TOKENS, 2 * KEY_WIDTH), bf16),
            jax.ShapeDtypeStruct((window, 1, limit), jnp.int32),
            jax.ShapeDtypeStruct((BLOCKS * KEY_VALUE_HEADS, PICKED_BLOCKS), jnp.int32),
        ),
        in_specs=[smem, vmem, vmem, vmem, vmem],
        out_specs=(vmem, vmem, smem, smem),
        scratch_shapes=[pltpu.SMEM((window,), jnp.int32)],
        name="prep",
    )(picks.transpose(0, 2, 1), keys, values, cosine, sine)

    near_k = lax.ppermute(rotated_keys, "ctx", behind)
    wanted = lax.all_to_all(table, "ctx", split_axis=0, concat_axis=0, tiled=True)
    wanted, near_k, near_v = lax.optimization_barrier((wanted, near_k, near_v))
    far_even = lax.ppermute(last, "ctx", [((i - 2 if i % 2 == 0 else i + 2) % window, i) for i in range(window)])

    answer = pl.pallas_call(
        gather_kernel,
        out_shape=jax.ShapeDtypeStruct((window, limit, 2, BLOCK_TOKENS, HEAD_SIZE), bf16),
        in_specs=[smem, vmem, vmem],
        out_specs=hbm,
        scratch_shapes=[pltpu.SemaphoreType.DMA((2, window, limit))],
        cost_estimate=pl.CostEstimate(flops=0, bytes_accessed=60 << 20, transcendentals=0),
        name="gather",
    )(wanted, rotated_keys, values)
    landed = lax.all_to_all(answer, "ctx", split_axis=0, concat_axis=0, tiled=True)
    landed = landed.reshape(window * limit, 2, BLOCK_TOKENS, HEAD_SIZE)

    band_flops = 4 * BLOCKS * QUERY_HEADS * BLOCK_TOKENS * LOCAL_BAND_SIZE * BLOCK_TOKENS * HEAD_SIZE
    full = (KEY_VALUE_HEADS, ROWS, HEAD_SIZE)

    def band(b, weight, *far):
        return pl.pallas_call(
            functools.partial(band_kernel, b),
            out_shape=(
                jax.ShapeDtypeStruct(full, bf16),
                jax.ShapeDtypeStruct(full, bf16),
                jax.ShapeDtypeStruct((ROWS, HEAD_SIZE), bf16),
            ),
            in_specs=[smem] + [vmem] * (7 + len(far)),
            out_specs=(vmem,) * 3,
            cost_estimate=pl.CostEstimate(flops=weight * band_flops, bytes_accessed=8 << 20, transcendentals=1 << 22),
            compiler_params=pltpu.CompilerParams(vmem_limit_bytes=30 << 20),
            name="band",
        )(me, queries, cosine, sine, near_k, near_v, rotated_keys, values, *far)

    second = band(1, 50)
    edge_k, edge_v, _ = lax.optimization_barrier((near_k, near_v, second[2]))
    edge = jnp.concatenate([edge_k[tokens - BLOCK_TOKENS :], edge_v[tokens - BLOCK_TOKENS :]], 1)
    far_odd = lax.ppermute(edge, "ctx", [(i ^ 1, i) for i in range(window)])
    first = band(0, 1, far_even, far_odd)

    count = BLOCKS * KEY_VALUE_HEADS
    narrow = (count, ROWS, HEAD_SIZE)
    return pl.pallas_call(
        picks_kernel,
        out_shape=jax.ShapeDtypeStruct((tokens, QUERY_HEADS * HEAD_SIZE), bf16),
        in_specs=[smem] + [hbm] * (1 + 3 * BLOCKS),
        out_specs=hbm,
        scratch_shapes=[
            pltpu.VMEM(narrow, bf16),
            pltpu.VMEM((count, PICKED_BLOCKS, 2, BLOCK_TOKENS, HEAD_SIZE), bf16),
            pltpu.VMEM(narrow, bf16),
            pltpu.VMEM((BLOCKS, ROWS, HEAD_SIZE), bf16),
            pltpu.VMEM((count, BLOCK_TOKENS, ROWS), bf16),
            pltpu.SemaphoreType.DMA((count, PICKED_BLOCKS + 2)),
            pltpu.SemaphoreType.DMA((count,)),
            pltpu.SemaphoreType.DMA((BLOCKS,)),
        ],
        cost_estimate=pl.CostEstimate(flops=2 * band_flops, bytes_accessed=16 << 20, transcendentals=1 << 22),
        compiler_params=pltpu.CompilerParams(vmem_limit_bytes=58 << 20),
        name="picks",
    )(slot, landed, *first, *second)


def solution(mesh):
    return jax.shard_map(
        shards,
        mesh=mesh,
        in_specs=(
            P(("groups", "ctx"), None),
            P(("groups", "ctx"), None),
            P(("groups", "ctx"), None),
            P(("groups", "ctx")),
            P(("groups", "ctx"), None, None),
        ),
        out_specs=P(("groups", "ctx"), None),
        check_vma=False,
    )
```

```python
import functools

import jax
import jax.numpy as jnp
import numpy as np
from jax import lax
from jax.experimental import pallas as pl
from jax.experimental.pallas import tpu as pltpu
from jax.sharding import PartitionSpec as P

QUERY_HEADS = 64
KEY_VALUE_HEADS = 8
HEAD_SIZE = 128
BLOCK_TOKENS = 128
LOCAL_BAND_SIZE = 4
PICKED_BLOCKS = 2
KEY_WIDTH = KEY_VALUE_HEADS * HEAD_SIZE
GROUP = QUERY_HEADS // KEY_VALUE_HEADS
ROWS = GROUP * BLOCK_TOKENS
PAIR = 2 * HEAD_SIZE
BLOCKS = 2

rope_base = 500000.0
masked_score = -1e30
score_factor = HEAD_SIZE ** (-0.5) * 1.4426950408889634

PARTS = 3

BAND_ROWS = 256
PICK_ROWS = 512
PICK_UNROLL = 8
PICK_AHEAD = 1

SMEM = pltpu.MemorySpace.SMEM


def frequencies():
    half = HEAD_SIZE // 2
    freq = rope_base ** (-(np.arange(half, dtype=np.float64) * 2.0) / HEAD_SIZE)
    return np.concatenate([freq, freq])[None, :].astype(np.float32)


def rotate(x, cosine, sine):
    wide = x.astype(jnp.float32)
    swapped = pltpu.roll(wide, HEAD_SIZE // 2, 1)
    return (wide * cosine + swapped * sine).astype(jnp.bfloat16)


def prep_kernel(
    limit, picks_ref, k_ref, v_ref, pos_ref, freq_ref, kr_ref, last_ref, cos_ref, sin_ref, table_ref, slot_ref, count_ref
):
    shards = table_ref.shape[0]

    @pl.loop(0, shards)
    def _(i):
        count_ref[i] = 0
        for r in range(limit):
            table_ref[i, 0, r] = -1

    @pl.loop(0, BLOCKS * KEY_VALUE_HEADS)
    def _(i):
        b = i // KEY_VALUE_HEADS
        h = i % KEY_VALUE_HEADS
        for p in range(PICKED_BLOCKS):
            pick = picks_ref[b, p, h]
            slot_ref[i, p] = -1

            @pl.when(pick >= 0)
            def _():
                owner = pick // BLOCKS
                rank = jnp.minimum(count_ref[owner], limit - 1)
                count_ref[owner] = rank + 1
                table_ref[owner, 0, rank] = pick % BLOCKS * KEY_VALUE_HEADS + h
                slot_ref[i, p] = owner * limit + rank

    spread = [
        jnp.broadcast_to(pos_ref[b : b + 1, :].astype(jnp.float32), (BLOCK_TOKENS, BLOCK_TOKENS)).T
        for b in range(BLOCKS)
    ]
    upper = lax.broadcasted_iota(jnp.int32, spread[0].shape, 1) >= HEAD_SIZE // 2
    angle = jnp.where(upper, spread[1], spread[0]) * freq_ref[...]
    cosines = jnp.cos(angle)
    sines = jnp.sin(angle)
    for b in range(BLOCKS):
        rows = slice(b * BLOCK_TOKENS, (b + 1) * BLOCK_TOKENS)
        cosine, sine = (jnp.where(upper == (b == 1), x, pltpu.roll(x, HEAD_SIZE // 2, 1)) for x in (cosines, sines))
        sine = jnp.where(upper, sine, -sine)
        cos_ref[rows, :] = cosine
        sin_ref[rows, :] = sine
        for h in range(KEY_VALUE_HEADS):
            cols = slice(h * HEAD_SIZE, (h + 1) * HEAD_SIZE)
            rotated = rotate(k_ref[rows, cols], cosine, sine)
            kr_ref[rows, cols] = rotated
            if b == BLOCKS - 1:
                last_ref[:, cols] = rotated
    last_ref[:, KEY_WIDTH:] = v_ref[(BLOCKS - 1) * BLOCK_TOKENS :, :]


def gather_kernel(wanted_ref, k_ref, v_ref, out_ref, sems):
    shards, _, limit = wanted_ref.shape

    def copies(i, r):
        entry = jnp.maximum(wanted_ref[i, 0, r], 0)
        rows = pl.ds(pl.multiple_of(entry // KEY_VALUE_HEADS * BLOCK_TOKENS, BLOCK_TOKENS), BLOCK_TOKENS)
        cols = pl.ds(pl.multiple_of(entry % KEY_VALUE_HEADS * HEAD_SIZE, HEAD_SIZE), HEAD_SIZE)
        return [
            pltpu.make_async_copy(src.at[rows, cols], out_ref.at[i, r, n], sems.at[n, i, r])
            for n, src in enumerate((k_ref, v_ref))
        ]

    @pl.loop(0, shards)
    def _(i):
        for r in range(limit):
            for copy in copies(i, r):
                copy.start()

    @pl.loop(0, shards)
    def _(i):
        for r in range(limit):
            for copy in copies(i, r):
                copy.wait()


def scores_of(query, key):
    return lax.dot_general(query, key, (((1,), (1,)), ((), ())), preferred_element_type=jnp.float32)


def summed(weight, value):
    both = jnp.concatenate([value, jnp.ones_like(value)], 1)
    out = jnp.dot(weight, both, preferred_element_type=jnp.float32)
    return out[:, :HEAD_SIZE], out[:, HEAD_SIZE:]


def band_kernel(b, me_ref, q_ref, cos_ref, sin_ref, nk_ref, nv_ref, k_ref, v_ref, *rest):
    far_refs = rest[:-3]
    qr_ref, acc_ref, sums_ref = rest[-3:]
    lane = lax.broadcasted_iota(jnp.int32, (BAND_ROWS, HEAD_SIZE), 1)
    sums_ref[...] = jnp.zeros_like(sums_ref)
    me = me_ref[0]
    row = lax.broadcasted_iota(jnp.int32, (BLOCK_TOKENS, BLOCK_TOKENS), 0)
    col = lax.broadcasted_iota(jnp.int32, (BLOCK_TOKENS, BLOCK_TOKENS), 1)
    causal = jnp.concatenate([col <= row] * (BAND_ROWS // BLOCK_TOKENS), 0)
    edge = (LOCAL_BAND_SIZE - 1) * BLOCK_TOKENS
    own = (b + 1) * BLOCK_TOKENS
    rows = slice(b * BLOCK_TOKENS, (b + 1) * BLOCK_TOKENS)

    def attend(start, h):
        at_key = pl.ds(pl.multiple_of(h * HEAD_SIZE, HEAD_SIZE), HEAD_SIZE)
        at_value = pl.ds(pl.multiple_of(KEY_WIDTH + h * HEAD_SIZE, HEAD_SIZE), HEAD_SIZE)
        keys = [nk_ref[:, at_key], k_ref[:own, at_key]]
        values = [nv_ref[:, at_key], v_ref[:own, at_key]]
        if far_refs:
            even_ref, odd_ref = far_refs
            odd = me % 2 == 1
            keys = [jnp.where(odd, odd_ref[:, at_key], even_ref[:, at_key])] + keys
            values = [jnp.where(odd, odd_ref[:, at_value], even_ref[:, at_value])] + values
        key = jnp.concatenate(keys, 0)
        value = jnp.concatenate(values, 0)
        query = q_ref[rows, pl.ds(pl.multiple_of(h * ROWS, ROWS), ROWS)]
        for first in range(0, ROWS, BAND_ROWS):
            part = slice(first, first + BAND_ROWS)
            rotated = jnp.concatenate(
                [
                    rotate(query[:, at : at + HEAD_SIZE], cos_ref[rows, :], sin_ref[rows, :])
                    for at in range(first, first + BAND_ROWS, HEAD_SIZE)
                ],
                0,
            )
            qr_ref[h, part, :] = rotated
            score = scores_of(rotated, key)
            before = score[:, :edge]
            if start:
                oldest = (me * BLOCKS + b - (LOCAL_BAND_SIZE - 1)) * BLOCK_TOKENS
                index = oldest + lax.broadcasted_iota(jnp.int32, before.shape, 1)
                before = jnp.where(index >= 0, before, masked_score)
            score = jnp.concatenate([before, jnp.where(causal, score[:, edge:], masked_score)], 1)
            top = jnp.max(score, -1, keepdims=True) * score_factor
            weight = jnp.exp2(score * score_factor - top)
            out, total = summed(weight.astype(jnp.bfloat16), value)
            acc_ref[h, part, :] = (out / total).astype(acc_ref.dtype)
            left = (jnp.log2(total) + top) * (1.0 / score_factor)
            sums = sums_ref[part, :].astype(jnp.float32)
            for n in range(PARTS):
                addend = left.astype(jnp.bfloat16).astype(jnp.float32)
                sums = jnp.where(lane == PARTS * h + n, addend, sums)
                left = left - addend
            sums_ref[part, :] = sums.astype(sums_ref.dtype)

    early = me * BLOCKS + b < LOCAL_BAND_SIZE - 1

    @pl.when(early)
    def _():
        pl.loop(0, KEY_VALUE_HEADS)(functools.partial(attend, True))

    @pl.when(jnp.logical_not(early))
    def _():
        pl.loop(0, KEY_VALUE_HEADS)(functools.partial(attend, False))


def picks_kernel(slot_ref, landed_hbm, *rest):
    band_hbm = rest[: 3 * BLOCKS]
    out_hbm, q_ref, piece_ref, acc_ref, sums_ref, out_ref, ins, outs, sums_sems = rest[3 * BLOCKS :]
    rounds = KEY_VALUE_HEADS // PICK_UNROLL

    def loads(b, h):
        i = b * KEY_VALUE_HEADS + h
        pairs = [(landed_hbm.at[jnp.maximum(slot_ref[i, p], 0)], piece_ref.at[i, p]) for p in range(PICKED_BLOCKS)]
        pairs += [(src.at[h], dst.at[i]) for src, dst in zip(band_hbm[3 * b : 3 * b + 2], (q_ref, acc_ref))]
        return [pltpu.make_async_copy(src, dst, ins.at[i, n]) for n, (src, dst) in enumerate(pairs)]

    def store(b, h):
        i = b * KEY_VALUE_HEADS + h
        rows = pl.ds(b * BLOCK_TOKENS, BLOCK_TOKENS)
        cols = pl.ds(pl.multiple_of(h * ROWS, ROWS), ROWS)
        return pltpu.make_async_copy(out_ref.at[i], out_hbm.at[rows, cols], outs.at[i])

    def start_round(b, j):
        for u in range(PICK_UNROLL):
            for copy in loads(b, j * PICK_UNROLL + u):
                copy.start()

    def sums_load(b):
        return pltpu.make_async_copy(band_hbm[3 * b + 2], sums_ref.at[b], sums_sems.at[b])

    def step(b, h):
        i = b * KEY_VALUE_HEADS + h
        bias = jnp.where(slot_ref[i, 0] >= 0, 0.0, masked_score)
        key = jnp.concatenate([piece_ref[i, p, 0] for p in range(PICKED_BLOCKS)], 0)
        lane = lax.broadcasted_iota(jnp.int32, key.shape, 1)
        minus = jnp.where((lane >= PARTS * h) & (lane < PARTS * h + PARTS), -1.0, 0.0).astype(key.dtype)
        key = jnp.concatenate([key, minus], 1)
        value = jnp.concatenate([piece_ref[i, p, 1] for p in range(PICKED_BLOCKS)], 0)
        for first in range(0, ROWS, PICK_ROWS):
            part = slice(first, first + PICK_ROWS)
            score = scores_of(jnp.concatenate([q_ref[i, part, :], sums_ref[b, part, :]], 1), key)
            best = jnp.max(score, -1, keepdims=True) * score_factor + bias
            top = jnp.maximum(jnp.broadcast_to(best, (PICK_ROWS, HEAD_SIZE)), 0.0)
            shift = top - bias
            weight = jnp.exp2(score * score_factor - jnp.concatenate([shift] * PICKED_BLOCKS, 1))
            fade = jnp.exp2(-top)
            out, total = summed(weight.astype(jnp.bfloat16), value)
            out = out + acc_ref[i, part, :].astype(jnp.float32) * fade
            result = (out / (total + fade)).astype(out_ref.dtype)
            for g in range(PICK_ROWS // BLOCK_TOKENS):
                at = slice(g * BLOCK_TOKENS, (g + 1) * BLOCK_TOKENS)
                out_ref[i, :, first + g * HEAD_SIZE : first + (g + 1) * HEAD_SIZE] = result[at]

    sums_load(0).start()
    for j in range(PICK_AHEAD):
        start_round(0, j)
    for b in range(1, BLOCKS):
        sums_load(b).start()

    for b in range(BLOCKS):
        sums_load(b).wait()

        @pl.loop(0, rounds)
        def _(j):
            @pl.when(j + PICK_AHEAD < rounds)
            def _():
                start_round(b, j + PICK_AHEAD)

            if b + 1 < BLOCKS:

                @pl.when(j + PICK_AHEAD >= rounds)
                def _():
                    start_round(b + 1, j + PICK_AHEAD - rounds)

            for u in range(PICK_UNROLL):
                for copy in loads(b, j * PICK_UNROLL + u):
                    copy.wait()

            for u in range(PICK_UNROLL):
                h = j * PICK_UNROLL + u
                step(b, h)
                store(b, h).start()

    for b in range(BLOCKS):
        for h in range(KEY_VALUE_HEADS):
            store(b, h).wait()


def shards(queries, keys, values, positions, picks):
    tokens = queries.shape[0]
    window = lax.axis_size("ctx")
    limit = max(1, BLOCKS * KEY_VALUE_HEADS * PICKED_BLOCKS // window)
    me = lax.axis_index("ctx").astype(jnp.int32).reshape(1)
    bf16 = jnp.bfloat16
    vmem = pl.BlockSpec(memory_space=pltpu.MemorySpace.VMEM)
    smem = pl.BlockSpec(memory_space=SMEM)
    hbm = pl.BlockSpec(memory_space=pl.ANY)

    behind = [((i - 1) % window, i) for i in range(window)]
    near_v = lax.ppermute(values, "ctx", behind)
    rotated_keys, last, cosine, sine, table, slot = pl.pallas_call(
        functools.partial(prep_kernel, limit),
        out_shape=(
            jax.ShapeDtypeStruct((tokens, KEY_WIDTH), bf16),
            jax.ShapeDtypeStruct((BLOCK_TOKENS, 2 * KEY_WIDTH), bf16),
            jax.ShapeDtypeStruct((tokens, HEAD_SIZE), jnp.float32),
            jax.ShapeDtypeStruct((tokens, HEAD_SIZE), jnp.float32),
            jax.ShapeDtypeStruct((window, 1, limit), jnp.int32),
            jax.ShapeDtypeStruct((BLOCKS * KEY_VALUE_HEADS, PICKED_BLOCKS), jnp.int32),
        ),
        in_specs=[smem, vmem, vmem, vmem, vmem],
        out_specs=(vmem, vmem, vmem, vmem, smem, smem),
        scratch_shapes=[pltpu.SMEM((window,), jnp.int32)],
        name="prep",
    )(picks.transpose(0, 2, 1), keys, values, positions.reshape(BLOCKS, BLOCK_TOKENS), jnp.asarray(frequencies()))

    near_k = lax.ppermute(rotated_keys, "ctx", behind)
    wanted = lax.all_to_all(table, "ctx", split_axis=0, concat_axis=0, tiled=True)
    wanted, near_k, near_v = lax.optimization_barrier((wanted, near_k, near_v))
    far_even = lax.ppermute(last, "ctx", [((i - 2) % window, i) for i in range(0, window, 2)])

    answer = pl.pallas_call(
        gather_kernel,
        out_shape=jax.ShapeDtypeStruct((window, limit, 2, BLOCK_TOKENS, HEAD_SIZE), bf16),
        in_specs=[smem, vmem, vmem],
        out_specs=hbm,
        scratch_shapes=[pltpu.SemaphoreType.DMA((2, window, limit))],
        cost_estimate=pl.CostEstimate(flops=0, bytes_accessed=60 << 20, transcendentals=0),
        name="gather",
    )(wanted, rotated_keys, values)
    landed = lax.all_to_all(answer, "ctx", split_axis=0, concat_axis=0, tiled=True)
    landed = landed.reshape(window * limit, 2, BLOCK_TOKENS, HEAD_SIZE)

    band_flops = 4 * BLOCKS * QUERY_HEADS * BLOCK_TOKENS * LOCAL_BAND_SIZE * BLOCK_TOKENS * HEAD_SIZE
    full = (KEY_VALUE_HEADS, ROWS, HEAD_SIZE)

    def band(b, weight, *far):
        return pl.pallas_call(
            functools.partial(band_kernel, b),
            out_shape=(
                jax.ShapeDtypeStruct(full, bf16),
                jax.ShapeDtypeStruct(full, bf16),
                jax.ShapeDtypeStruct((ROWS, HEAD_SIZE), bf16),
            ),
            in_specs=[smem] + [vmem] * (7 + len(far)),
            out_specs=(vmem,) * 3,
            cost_estimate=pl.CostEstimate(flops=weight * band_flops, bytes_accessed=8 << 20, transcendentals=1 << 22),
            compiler_params=pltpu.CompilerParams(vmem_limit_bytes=30 << 20),
            name="band",
        )(me, queries, cosine, sine, near_k, near_v, rotated_keys, values, *far)

    second = band(1, 50)
    edge_k, edge_v, _ = lax.optimization_barrier((near_k, near_v, second[2]))
    edge = jnp.concatenate([edge_k[tokens - BLOCK_TOKENS :], edge_v[tokens - BLOCK_TOKENS :]], 1)
    far_odd = lax.ppermute(edge, "ctx", [(i ^ 1, i) for i in range(window)])
    first = band(0, 1, far_even, far_odd)

    count = BLOCKS * KEY_VALUE_HEADS
    narrow = (count, ROWS, HEAD_SIZE)
    return pl.pallas_call(
        picks_kernel,
        out_shape=jax.ShapeDtypeStruct((tokens, QUERY_HEADS * HEAD_SIZE), bf16),
        in_specs=[smem] + [hbm] * (1 + 3 * BLOCKS),
        out_specs=hbm,
        scratch_shapes=[
            pltpu.VMEM(narrow, bf16),
            pltpu.VMEM((count, PICKED_BLOCKS, 2, BLOCK_TOKENS, HEAD_SIZE), bf16),
            pltpu.VMEM(narrow, bf16),
            pltpu.VMEM((BLOCKS, ROWS, HEAD_SIZE), bf16),
            pltpu.VMEM((count, BLOCK_TOKENS, ROWS), bf16),
            pltpu.SemaphoreType.DMA((count, PICKED_BLOCKS + 2)),
            pltpu.SemaphoreType.DMA((count,)),
            pltpu.SemaphoreType.DMA((BLOCKS,)),
        ],
        cost_estimate=pl.CostEstimate(flops=2 * band_flops, bytes_accessed=16 << 20, transcendentals=1 << 22),
        compiler_params=pltpu.CompilerParams(vmem_limit_bytes=58 << 20),
        name="picks",
    )(slot, landed, *first, *second)


def solution(mesh):
    return jax.shard_map(
        shards,
        mesh=mesh,
        in_specs=(
            P(("groups", "ctx"), None),
            P(("groups", "ctx"), None),
            P(("groups", "ctx"), None),
            P(("groups", "ctx")),
            P(("groups", "ctx"), None, None),
        ),
        out_specs=P(("groups", "ctx"), None),
        check_vma=False,
    )
```

```python
import functools

import jax
import jax.numpy as jnp
import numpy as np
from jax import lax
from jax.experimental import pallas as pl
from jax.experimental.pallas import tpu as pltpu
from jax.sharding import PartitionSpec as P

QUERY_HEADS = 64
KEY_VALUE_HEADS = 8
HEAD_SIZE = 128
BLOCK_TOKENS = 128
LOCAL_BAND_SIZE = 4
PICKED_BLOCKS = 2
KEY_WIDTH = KEY_VALUE_HEADS * HEAD_SIZE
GROUP = QUERY_HEADS // KEY_VALUE_HEADS
ROWS = GROUP * BLOCK_TOKENS
PAIR = 2 * HEAD_SIZE
BLOCKS = 2

rope_base = 500000.0
masked_score = -1e30
score_factor = HEAD_SIZE ** (-0.5) * 1.4426950408889634

PARTS = 3

BAND_ROWS = 256
PICK_ROWS = 512
PICK_UNROLL = 8
PICK_AHEAD = 1

SMEM = pltpu.MemorySpace.SMEM


def frequencies():
    half = HEAD_SIZE // 2
    freq = rope_base ** (-(np.arange(half, dtype=np.float64) * 2.0) / HEAD_SIZE)
    return np.concatenate([freq, freq])[None, :].astype(np.float32)


def rotate(x, cosine, sine):
    wide = x.astype(jnp.float32)
    swapped = pltpu.roll(wide, HEAD_SIZE // 2, 1)
    return (wide * cosine + swapped * sine).astype(jnp.bfloat16)


def prep_kernel(
    limit, picks_ref, k_ref, v_hbm, pos_ref, freq_ref, kr_ref, last_ref, cos_ref, sin_ref, table_ref, slot_ref, count_ref, sem
):
    shards = table_ref.shape[0]
    tail = pltpu.make_async_copy(
        v_hbm.at[pl.ds((BLOCKS - 1) * BLOCK_TOKENS, BLOCK_TOKENS), :], last_ref.at[:, pl.ds(KEY_WIDTH, KEY_WIDTH)], sem
    )
    tail.start()

    @pl.loop(0, shards)
    def _(i):
        count_ref[i] = 0
        for r in range(limit):
            table_ref[i, 0, r] = -1

    @pl.loop(0, BLOCKS * KEY_VALUE_HEADS)
    def _(i):
        b = i // KEY_VALUE_HEADS
        h = i % KEY_VALUE_HEADS
        for p in range(PICKED_BLOCKS):
            pick = picks_ref[b, p, h]
            slot_ref[i, p] = -1

            @pl.when(pick >= 0)
            def _():
                owner = pick // BLOCKS
                rank = jnp.minimum(count_ref[owner], limit - 1)
                count_ref[owner] = rank + 1
                table_ref[owner, 0, rank] = pick % BLOCKS * KEY_VALUE_HEADS + h
                slot_ref[i, p] = owner * limit + rank

    spread = [
        jnp.broadcast_to(pos_ref[b : b + 1, :].astype(jnp.float32), (BLOCK_TOKENS, BLOCK_TOKENS)).T
        for b in range(BLOCKS)
    ]
    upper = lax.broadcasted_iota(jnp.int32, spread[0].shape, 1) >= HEAD_SIZE // 2
    angle = jnp.where(upper, spread[1], spread[0]) * freq_ref[...]
    cosines = jnp.cos(angle)
    sines = jnp.sin(angle)
    for b in range(BLOCKS):
        rows = slice(b * BLOCK_TOKENS, (b + 1) * BLOCK_TOKENS)
        cosine, sine = (jnp.where(upper == (b == 1), x, pltpu.roll(x, HEAD_SIZE // 2, 1)) for x in (cosines, sines))
        sine = jnp.where(upper, sine, -sine)
        cos_ref[rows, :] = cosine
        sin_ref[rows, :] = sine
        for h in range(KEY_VALUE_HEADS):
            cols = slice(h * HEAD_SIZE, (h + 1) * HEAD_SIZE)
            rotated = rotate(k_ref[rows, cols], cosine, sine)
            kr_ref[rows, cols] = rotated
            if b == BLOCKS - 1:
                last_ref[:, cols] = rotated
    tail.wait()


def gather_kernel(wanted_ref, k_ref, v_ref, out_ref, sems):
    shards, _, limit = wanted_ref.shape

    def copies(i, r):
        entry = jnp.maximum(wanted_ref[i, 0, r], 0)
        rows = pl.ds(pl.multiple_of(entry // KEY_VALUE_HEADS * BLOCK_TOKENS, BLOCK_TOKENS), BLOCK_TOKENS)
        cols = pl.ds(pl.multiple_of(entry % KEY_VALUE_HEADS * HEAD_SIZE, HEAD_SIZE), HEAD_SIZE)
        return [
            pltpu.make_async_copy(src.at[rows, cols], out_ref.at[i, r, n], sems.at[n, i, r])
            for n, src in enumerate((k_ref, v_ref))
        ]

    @pl.loop(0, shards)
    def _(i):
        for r in range(limit):
            for copy in copies(i, r):
                copy.start()

    @pl.loop(0, shards)
    def _(i):
        for r in range(limit):
            for copy in copies(i, r):
                copy.wait()


def scores_of(query, key):
    return lax.dot_general(query, key, (((1,), (1,)), ((), ())), preferred_element_type=jnp.float32)


def summed(weight, value):
    both = jnp.concatenate([value, jnp.ones_like(value)], 1)
    out = jnp.dot(weight, both, preferred_element_type=jnp.float32)
    return out[:, :HEAD_SIZE], out[:, HEAD_SIZE:]


def band_kernel(b, me_ref, q_ref, cos_ref, sin_ref, nk_ref, nv_ref, k_ref, v_ref, *rest):
    far_refs = rest[:-3]
    qr_ref, acc_ref, sums_ref = rest[-3:]
    lane = lax.broadcasted_iota(jnp.int32, (BAND_ROWS, HEAD_SIZE), 1)
    sums_ref[...] = jnp.zeros_like(sums_ref)
    me = me_ref[0]
    row = lax.broadcasted_iota(jnp.int32, (BLOCK_TOKENS, BLOCK_TOKENS), 0)
    col = lax.broadcasted_iota(jnp.int32, (BLOCK_TOKENS, BLOCK_TOKENS), 1)
    causal = jnp.concatenate([col <= row] * (BAND_ROWS // BLOCK_TOKENS), 0)
    edge = (LOCAL_BAND_SIZE - 1) * BLOCK_TOKENS
    own = (b + 1) * BLOCK_TOKENS
    rows = slice(b * BLOCK_TOKENS, (b + 1) * BLOCK_TOKENS)

    def attend(start, h):
        at_key = pl.ds(pl.multiple_of(h * HEAD_SIZE, HEAD_SIZE), HEAD_SIZE)
        at_value = pl.ds(pl.multiple_of(KEY_WIDTH + h * HEAD_SIZE, HEAD_SIZE), HEAD_SIZE)
        keys = [nk_ref[:, at_key], k_ref[:own, at_key]]
        values = [nv_ref[:, at_key], v_ref[:own, at_key]]
        if far_refs:
            even_ref, odd_ref = far_refs
            odd = me % 2 == 1
            keys = [jnp.where(odd, odd_ref[:, at_key], even_ref[:, at_key])] + keys
            values = [jnp.where(odd, odd_ref[:, at_value], even_ref[:, at_value])] + values
        key = jnp.concatenate(keys, 0)
        value = jnp.concatenate(values, 0)
        query = q_ref[rows, pl.ds(pl.multiple_of(h * ROWS, ROWS), ROWS)]
        for first in range(0, ROWS, BAND_ROWS):
            part = slice(first, first + BAND_ROWS)
            rotated = jnp.concatenate(
                [
                    rotate(query[:, at : at + HEAD_SIZE], cos_ref[rows, :], sin_ref[rows, :])
                    for at in range(first, first + BAND_ROWS, HEAD_SIZE)
                ],
                0,
            )
            qr_ref[h, part, :] = rotated
            score = scores_of(rotated, key)
            before = score[:, :edge]
            if start:
                oldest = (me * BLOCKS + b - (LOCAL_BAND_SIZE - 1)) * BLOCK_TOKENS
                index = oldest + lax.broadcasted_iota(jnp.int32, before.shape, 1)
                before = jnp.where(index >= 0, before, masked_score)
            score = jnp.concatenate([before, jnp.where(causal, score[:, edge:], masked_score)], 1)
            top = jnp.max(score, -1, keepdims=True) * score_factor
            weight = jnp.exp2(score * score_factor - top)
            out, total = summed(weight.astype(jnp.bfloat16), value)
            acc_ref[h, part, :] = (out / total).astype(acc_ref.dtype)
            left = (jnp.log2(total) + top) * (1.0 / score_factor)
            sums = sums_ref[part, :].astype(jnp.float32)
            for n in range(PARTS):
                addend = left.astype(jnp.bfloat16).astype(jnp.float32)
                sums = jnp.where(lane == PARTS * h + n, addend, sums)
                left = left - addend
            sums_ref[part, :] = sums.astype(sums_ref.dtype)

    early = me * BLOCKS + b < LOCAL_BAND_SIZE - 1

    @pl.when(early)
    def _():
        pl.loop(0, KEY_VALUE_HEADS)(functools.partial(attend, True))

    @pl.when(jnp.logical_not(early))
    def _():
        pl.loop(0, KEY_VALUE_HEADS)(functools.partial(attend, False))


def picks_kernel(slot_ref, landed_hbm, *rest):
    band_hbm = rest[: 3 * BLOCKS]
    out_hbm, q_ref, piece_ref, acc_ref, sums_ref, out_ref, ins, outs, sums_sems = rest[3 * BLOCKS :]
    rounds = KEY_VALUE_HEADS // PICK_UNROLL

    def loads(b, h):
        i = b * KEY_VALUE_HEADS + h
        pairs = [(landed_hbm.at[jnp.maximum(slot_ref[i, p], 0)], piece_ref.at[i, p]) for p in range(PICKED_BLOCKS)]
        pairs += [(src.at[h], dst.at[i]) for src, dst in zip(band_hbm[3 * b : 3 * b + 2], (q_ref, acc_ref))]
        return [pltpu.make_async_copy(src, dst, ins.at[i, n]) for n, (src, dst) in enumerate(pairs)]

    def store(b, h):
        i = b * KEY_VALUE_HEADS + h
        rows = pl.ds(b * BLOCK_TOKENS, BLOCK_TOKENS)
        cols = pl.ds(pl.multiple_of(h * ROWS, ROWS), ROWS)
        return pltpu.make_async_copy(out_ref.at[i], out_hbm.at[rows, cols], outs.at[i])

    def start_round(b, j):
        for u in range(PICK_UNROLL):
            for copy in loads(b, j * PICK_UNROLL + u):
                copy.start()

    def sums_load(b):
        return pltpu.make_async_copy(band_hbm[3 * b + 2], sums_ref.at[b], sums_sems.at[b])

    def step(b, h):
        i = b * KEY_VALUE_HEADS + h
        bias = jnp.where(slot_ref[i, 0] >= 0, 0.0, masked_score)
        key = jnp.concatenate([piece_ref[i, p, 0] for p in range(PICKED_BLOCKS)], 0)
        lane = lax.broadcasted_iota(jnp.int32, key.shape, 1)
        minus = jnp.where((lane >= PARTS * h) & (lane < PARTS * h + PARTS), -1.0, 0.0).astype(key.dtype)
        key = jnp.concatenate([key, minus], 1)
        value = jnp.concatenate([piece_ref[i, p, 1] for p in range(PICKED_BLOCKS)], 0)
        for first in range(0, ROWS, PICK_ROWS):
            part = slice(first, first + PICK_ROWS)
            score = scores_of(jnp.concatenate([q_ref[i, part, :], sums_ref[b, part, :]], 1), key)
            best = jnp.max(score, -1, keepdims=True) * score_factor + bias
            top = jnp.maximum(jnp.broadcast_to(best, (PICK_ROWS, HEAD_SIZE)), 0.0)
            shift = top - bias
            weight = jnp.exp2(score * score_factor - jnp.concatenate([shift] * PICKED_BLOCKS, 1))
            fade = jnp.exp2(-top)
            out, total = summed(weight.astype(jnp.bfloat16), value)
            out = out + acc_ref[i, part, :].astype(jnp.float32) * fade
            result = (out / (total + fade)).astype(out_ref.dtype)
            for g in range(PICK_ROWS // BLOCK_TOKENS):
                at = slice(g * BLOCK_TOKENS, (g + 1) * BLOCK_TOKENS)
                out_ref[i, :, first + g * HEAD_SIZE : first + (g + 1) * HEAD_SIZE] = result[at]

    sums_load(0).start()
    for j in range(PICK_AHEAD):
        start_round(0, j)
    for b in range(1, BLOCKS):
        sums_load(b).start()

    for b in range(BLOCKS):
        sums_load(b).wait()

        @pl.loop(0, rounds)
        def _(j):
            @pl.when(j + PICK_AHEAD < rounds)
            def _():
                start_round(b, j + PICK_AHEAD)

            if b + 1 < BLOCKS:

                @pl.when(j + PICK_AHEAD >= rounds)
                def _():
                    start_round(b + 1, j + PICK_AHEAD - rounds)

            for u in range(PICK_UNROLL):
                for copy in loads(b, j * PICK_UNROLL + u):
                    copy.wait()

            for u in range(PICK_UNROLL):
                h = j * PICK_UNROLL + u
                step(b, h)
                store(b, h).start()

    for b in range(BLOCKS):
        for h in range(KEY_VALUE_HEADS):
            store(b, h).wait()


def shards(queries, keys, values, positions, picks):
    tokens = queries.shape[0]
    window = lax.axis_size("ctx")
    limit = max(1, BLOCKS * KEY_VALUE_HEADS * PICKED_BLOCKS // window)
    me = lax.axis_index("ctx").astype(jnp.int32).reshape(1)
    bf16 = jnp.bfloat16
    vmem = pl.BlockSpec(memory_space=pltpu.MemorySpace.VMEM)
    smem = pl.BlockSpec(memory_space=SMEM)
    hbm = pl.BlockSpec(memory_space=pl.ANY)

    behind = [((i - 1) % window, i) for i in range(window)]
    near_v = lax.ppermute(values, "ctx", behind)
    rotated_keys, last, cosine, sine, table, slot = pl.pallas_call(
        functools.partial(prep_kernel, limit),
        out_shape=(
            jax.ShapeDtypeStruct((tokens, KEY_WIDTH), bf16),
            jax.ShapeDtypeStruct((BLOCK_TOKENS, 2 * KEY_WIDTH), bf16),
            jax.ShapeDtypeStruct((tokens, HEAD_SIZE), jnp.float32),
            jax.ShapeDtypeStruct((tokens, HEAD_SIZE), jnp.float32),
            jax.ShapeDtypeStruct((window, 1, limit), jnp.int32),
            jax.ShapeDtypeStruct((BLOCKS * KEY_VALUE_HEADS, PICKED_BLOCKS), jnp.int32),
        ),
        in_specs=[smem, vmem, hbm, vmem, vmem],
        out_specs=(vmem, vmem, vmem, vmem, smem, smem),
        scratch_shapes=[pltpu.SMEM((window,), jnp.int32), pltpu.SemaphoreType.DMA],
        name="prep",
    )(picks.transpose(0, 2, 1), keys, values, positions.reshape(BLOCKS, BLOCK_TOKENS), jnp.asarray(frequencies()))

    near_k = lax.ppermute(rotated_keys, "ctx", behind)
    wanted = lax.all_to_all(table, "ctx", split_axis=0, concat_axis=0, tiled=True)
    wanted, near_k, near_v = lax.optimization_barrier((wanted, near_k, near_v))
    far_even = lax.ppermute(last, "ctx", [((i - 2) % window, i) for i in range(0, window, 2)])

    answer = pl.pallas_call(
        gather_kernel,
        out_shape=jax.ShapeDtypeStruct((window, limit, 2, BLOCK_TOKENS, HEAD_SIZE), bf16),
        in_specs=[smem, vmem, vmem],
        out_specs=hbm,
        scratch_shapes=[pltpu.SemaphoreType.DMA((2, window, limit))],
        cost_estimate=pl.CostEstimate(flops=0, bytes_accessed=60 << 20, transcendentals=0),
        name="gather",
    )(wanted, rotated_keys, values)
    landed = lax.all_to_all(answer, "ctx", split_axis=0, concat_axis=0, tiled=True)
    landed = landed.reshape(window * limit, 2, BLOCK_TOKENS, HEAD_SIZE)

    band_flops = 4 * BLOCKS * QUERY_HEADS * BLOCK_TOKENS * LOCAL_BAND_SIZE * BLOCK_TOKENS * HEAD_SIZE
    full = (KEY_VALUE_HEADS, ROWS, HEAD_SIZE)

    def band(b, weight, *far):
        return pl.pallas_call(
            functools.partial(band_kernel, b),
            out_shape=(
                jax.ShapeDtypeStruct(full, bf16),
                jax.ShapeDtypeStruct(full, bf16),
                jax.ShapeDtypeStruct((ROWS, HEAD_SIZE), bf16),
            ),
            in_specs=[smem] + [vmem] * (7 + len(far)),
            out_specs=(vmem,) * 3,
            cost_estimate=pl.CostEstimate(flops=weight * band_flops, bytes_accessed=8 << 20, transcendentals=1 << 22),
            compiler_params=pltpu.CompilerParams(vmem_limit_bytes=30 << 20),
            name="band",
        )(me, queries, cosine, sine, near_k, near_v, rotated_keys, values, *far)

    second = band(1, 50)
    edge_k, edge_v, _ = lax.optimization_barrier((near_k, near_v, second[2]))
    edge = jnp.concatenate([edge_k[tokens - BLOCK_TOKENS :], edge_v[tokens - BLOCK_TOKENS :]], 1)
    far_odd = lax.ppermute(edge, "ctx", [(i ^ 1, i) for i in range(window)])
    first = band(0, 1, far_even, far_odd)

    count = BLOCKS * KEY_VALUE_HEADS
    narrow = (count, ROWS, HEAD_SIZE)
    return pl.pallas_call(
        picks_kernel,
        out_shape=jax.ShapeDtypeStruct((tokens, QUERY_HEADS * HEAD_SIZE), bf16),
        in_specs=[smem] + [hbm] * (1 + 3 * BLOCKS),
        out_specs=hbm,
        scratch_shapes=[
            pltpu.VMEM(narrow, bf16),
            pltpu.VMEM((count, PICKED_BLOCKS, 2, BLOCK_TOKENS, HEAD_SIZE), bf16),
            pltpu.VMEM(narrow, bf16),
            pltpu.VMEM((BLOCKS, ROWS, HEAD_SIZE), bf16),
            pltpu.VMEM((count, BLOCK_TOKENS, ROWS), bf16),
            pltpu.SemaphoreType.DMA((count, PICKED_BLOCKS + 2)),
            pltpu.SemaphoreType.DMA((count,)),
            pltpu.SemaphoreType.DMA((BLOCKS,)),
        ],
        cost_estimate=pl.CostEstimate(flops=2 * band_flops, bytes_accessed=16 << 20, transcendentals=1 << 22),
        compiler_params=pltpu.CompilerParams(vmem_limit_bytes=58 << 20),
        name="picks",
    )(slot, landed, *first, *second)


def solution(mesh):
    return jax.shard_map(
        shards,
        mesh=mesh,
        in_specs=(
            P(("groups", "ctx"), None),
            P(("groups", "ctx"), None),
            P(("groups", "ctx"), None),
            P(("groups", "ctx")),
            P(("groups", "ctx"), None, None),
        ),
        out_specs=P(("groups", "ctx"), None),
        check_vma=False,
    )
```

```python
import functools

import jax
import jax.numpy as jnp
import numpy as np
from jax import lax
from jax.experimental import pallas as pl
from jax.experimental.pallas import tpu as pltpu
from jax.sharding import PartitionSpec as P

QUERY_HEADS = 64
KEY_VALUE_HEADS = 8
HEAD_SIZE = 128
BLOCK_TOKENS = 128
LOCAL_BAND_SIZE = 4
PICKED_BLOCKS = 2
KEY_WIDTH = KEY_VALUE_HEADS * HEAD_SIZE
GROUP = QUERY_HEADS // KEY_VALUE_HEADS
ROWS = GROUP * BLOCK_TOKENS
PAIR = 2 * HEAD_SIZE
BLOCKS = 2

rope_base = 500000.0
masked_score = -1e30
score_factor = HEAD_SIZE ** (-0.5) * 1.4426950408889634

PARTS = 3

BAND_ROWS = 256
PICK_ROWS = 256
PICK_UNROLL = 8
PICK_AHEAD = 1

SMEM = pltpu.MemorySpace.SMEM


def frequencies():
    half = HEAD_SIZE // 2
    freq = rope_base ** (-(np.arange(half, dtype=np.float64) * 2.0) / HEAD_SIZE)
    return np.concatenate([freq, freq])[None, :].astype(np.float32)


def rotate(x, cosine, sine):
    wide = x.astype(jnp.float32)
    swapped = pltpu.roll(wide, HEAD_SIZE // 2, 1)
    return (wide * cosine + swapped * sine).astype(jnp.bfloat16)


def prep_kernel(
    limit, picks_ref, k_ref, v_hbm, pos_ref, freq_ref, kr_ref, last_ref, cos_ref, sin_ref, table_ref, slot_ref, count_ref, sem
):
    shards = table_ref.shape[0]
    tail = pltpu.make_async_copy(
        v_hbm.at[pl.ds((BLOCKS - 1) * BLOCK_TOKENS, BLOCK_TOKENS), :], last_ref.at[:, pl.ds(KEY_WIDTH, KEY_WIDTH)], sem
    )
    tail.start()

    @pl.loop(0, shards)
    def _(i):
        count_ref[i] = 0
        for r in range(limit):
            table_ref[i, 0, r] = -1

    @pl.loop(0, BLOCKS * KEY_VALUE_HEADS)
    def _(i):
        b = i // KEY_VALUE_HEADS
        h = i % KEY_VALUE_HEADS
        for p in range(PICKED_BLOCKS):
            pick = picks_ref[b, p, h]
            slot_ref[i, p] = -1

            @pl.when(pick >= 0)
            def _():
                owner = pick // BLOCKS
                rank = jnp.minimum(count_ref[owner], limit - 1)
                count_ref[owner] = rank + 1
                table_ref[owner, 0, rank] = pick % BLOCKS * KEY_VALUE_HEADS + h
                slot_ref[i, p] = owner * limit + rank

    spread = [
        jnp.broadcast_to(pos_ref[b : b + 1, :].astype(jnp.float32), (BLOCK_TOKENS, BLOCK_TOKENS)).T
        for b in range(BLOCKS)
    ]
    upper = lax.broadcasted_iota(jnp.int32, spread[0].shape, 1) >= HEAD_SIZE // 2
    angle = jnp.where(upper, spread[1], spread[0]) * freq_ref[...]
    cosines = jnp.cos(angle)
    sines = jnp.sin(angle)
    for b in range(BLOCKS):
        rows = slice(b * BLOCK_TOKENS, (b + 1) * BLOCK_TOKENS)
        cosine, sine = (jnp.where(upper == (b == 1), x, pltpu.roll(x, HEAD_SIZE // 2, 1)) for x in (cosines, sines))
        sine = jnp.where(upper, sine, -sine)
        cos_ref[rows, :] = cosine
        sin_ref[rows, :] = sine
        for h in range(KEY_VALUE_HEADS):
            cols = slice(h * HEAD_SIZE, (h + 1) * HEAD_SIZE)
            rotated = rotate(k_ref[rows, cols], cosine, sine)
            kr_ref[rows, cols] = rotated
            if b == BLOCKS - 1:
                last_ref[:, cols] = rotated
    tail.wait()


def gather_kernel(wanted_ref, k_ref, v_ref, out_ref, sems):
    shards, _, limit = wanted_ref.shape

    def copies(i, r):
        entry = jnp.maximum(wanted_ref[i, 0, r], 0)
        rows = pl.ds(pl.multiple_of(entry // KEY_VALUE_HEADS * BLOCK_TOKENS, BLOCK_TOKENS), BLOCK_TOKENS)
        cols = pl.ds(pl.multiple_of(entry % KEY_VALUE_HEADS * HEAD_SIZE, HEAD_SIZE), HEAD_SIZE)
        return [
            pltpu.make_async_copy(src.at[rows, cols], out_ref.at[i, r, n], sems.at[n, i, r])
            for n, src in enumerate((k_ref, v_ref))
        ]

    @pl.loop(0, shards)
    def _(i):
        for r in range(limit):
            for copy in copies(i, r):
                copy.start()

    @pl.loop(0, shards)
    def _(i):
        for r in range(limit):
            for copy in copies(i, r):
                copy.wait()


def scores_of(query, key):
    return lax.dot_general(query, key, (((1,), (1,)), ((), ())), preferred_element_type=jnp.float32)


def summed(weight, value):
    both = jnp.concatenate([value, jnp.ones_like(value)], 1)
    out = jnp.dot(weight, both, preferred_element_type=jnp.float32)
    return out[:, :HEAD_SIZE], out[:, HEAD_SIZE:]


def band_kernel(b, me_ref, q_ref, cos_ref, sin_ref, nk_ref, nv_ref, k_ref, v_ref, *rest):
    far_refs = rest[:-3]
    qr_ref, acc_ref, sums_ref = rest[-3:]
    lane = lax.broadcasted_iota(jnp.int32, (BAND_ROWS, HEAD_SIZE), 1)
    sums_ref[...] = jnp.zeros_like(sums_ref)
    me = me_ref[0]
    row = lax.broadcasted_iota(jnp.int32, (BLOCK_TOKENS, BLOCK_TOKENS), 0)
    col = lax.broadcasted_iota(jnp.int32, (BLOCK_TOKENS, BLOCK_TOKENS), 1)
    causal = jnp.concatenate([col <= row] * (BAND_ROWS // BLOCK_TOKENS), 0)
    edge = (LOCAL_BAND_SIZE - 1) * BLOCK_TOKENS
    own = (b + 1) * BLOCK_TOKENS
    rows = slice(b * BLOCK_TOKENS, (b + 1) * BLOCK_TOKENS)

    def attend(start, h):
        at_key = pl.ds(pl.multiple_of(h * HEAD_SIZE, HEAD_SIZE), HEAD_SIZE)
        at_value = pl.ds(pl.multiple_of(KEY_WIDTH + h * HEAD_SIZE, HEAD_SIZE), HEAD_SIZE)
        keys = [nk_ref[:, at_key], k_ref[:own, at_key]]
        values = [nv_ref[:, at_key], v_ref[:own, at_key]]
        if far_refs:
            even_ref, odd_ref = far_refs
            odd = me % 2 == 1
            keys = [jnp.where(odd, odd_ref[:, at_key], even_ref[:, at_key])] + keys
            values = [jnp.where(odd, odd_ref[:, at_value], even_ref[:, at_value])] + values
        key = jnp.concatenate(keys, 0)
        value = jnp.concatenate(values, 0)
        query = q_ref[rows, pl.ds(pl.multiple_of(h * ROWS, ROWS), ROWS)]
        for first in range(0, ROWS, BAND_ROWS):
            part = slice(first, first + BAND_ROWS)
            rotated = jnp.concatenate(
                [
                    rotate(query[:, at : at + HEAD_SIZE], cos_ref[rows, :], sin_ref[rows, :])
                    for at in range(first, first + BAND_ROWS, HEAD_SIZE)
                ],
                0,
            )
            qr_ref[h, part, :] = rotated
            score = scores_of(rotated, key)
            before = score[:, :edge]
            if start:
                oldest = (me * BLOCKS + b - (LOCAL_BAND_SIZE - 1)) * BLOCK_TOKENS
                index = oldest + lax.broadcasted_iota(jnp.int32, before.shape, 1)
                before = jnp.where(index >= 0, before, masked_score)
            score = jnp.concatenate([before, jnp.where(causal, score[:, edge:], masked_score)], 1)
            top = jnp.max(score, -1, keepdims=True) * score_factor
            weight = jnp.exp2(score * score_factor - top)
            out, total = summed(weight.astype(jnp.bfloat16), value)
            acc_ref[h, part, :] = (out / total).astype(acc_ref.dtype)
            left = (jnp.log2(total) + top) * (1.0 / score_factor)
            sums = sums_ref[part, :].astype(jnp.float32)
            for n in range(PARTS):
                addend = left.astype(jnp.bfloat16).astype(jnp.float32)
                sums = jnp.where(lane == PARTS * h + n, addend, sums)
                left = left - addend
            sums_ref[part, :] = sums.astype(sums_ref.dtype)

    early = me * BLOCKS + b < LOCAL_BAND_SIZE - 1

    @pl.when(early)
    def _():
        pl.loop(0, KEY_VALUE_HEADS)(functools.partial(attend, True))

    @pl.when(jnp.logical_not(early))
    def _():
        pl.loop(0, KEY_VALUE_HEADS)(functools.partial(attend, False))


def picks_kernel(slot_ref, landed_hbm, *rest):
    band_hbm = rest[: 3 * BLOCKS]
    out_hbm, q_ref, piece_ref, acc_ref, sums_ref, out_ref, ins, outs, sums_sems = rest[3 * BLOCKS :]
    rounds = KEY_VALUE_HEADS // PICK_UNROLL

    def loads(b, h):
        i = b * KEY_VALUE_HEADS + h
        pairs = [(landed_hbm.at[jnp.maximum(slot_ref[i, p], 0)], piece_ref.at[i, p]) for p in range(PICKED_BLOCKS)]
        pairs += [(src.at[h], dst.at[i]) for src, dst in zip(band_hbm[3 * b : 3 * b + 2], (q_ref, acc_ref))]
        return [pltpu.make_async_copy(src, dst, ins.at[i, n]) for n, (src, dst) in enumerate(pairs)]

    def store(b, h):
        i = b * KEY_VALUE_HEADS + h
        rows = pl.ds(b * BLOCK_TOKENS, BLOCK_TOKENS)
        cols = pl.ds(pl.multiple_of(h * ROWS, ROWS), ROWS)
        return pltpu.make_async_copy(out_ref.at[i], out_hbm.at[rows, cols], outs.at[i])

    def start_round(b, j):
        for u in range(PICK_UNROLL):
            for copy in loads(b, j * PICK_UNROLL + u):
                copy.start()

    def sums_load(b):
        return pltpu.make_async_copy(band_hbm[3 * b + 2], sums_ref.at[b], sums_sems.at[b])

    def step(b, h):
        i = b * KEY_VALUE_HEADS + h
        bias = jnp.where(slot_ref[i, 0] >= 0, 0.0, masked_score)
        key = jnp.concatenate([piece_ref[i, p, 0] for p in range(PICKED_BLOCKS)], 0)
        lane = lax.broadcasted_iota(jnp.int32, key.shape, 1)
        minus = jnp.where((lane >= PARTS * h) & (lane < PARTS * h + PARTS), -1.0, 0.0).astype(key.dtype)
        key = jnp.concatenate([key, minus], 1)
        value = jnp.concatenate([piece_ref[i, p, 1] for p in range(PICKED_BLOCKS)], 0)
        for first in range(0, ROWS, PICK_ROWS):
            part = slice(first, first + PICK_ROWS)
            score = scores_of(jnp.concatenate([q_ref[i, part, :], sums_ref[b, part, :]], 1), key)
            best = jnp.max(score, -1, keepdims=True) * score_factor + bias
            top = jnp.maximum(jnp.broadcast_to(best, (PICK_ROWS, HEAD_SIZE)), 0.0)
            shift = top - bias
            weight = jnp.exp2(score * score_factor - jnp.concatenate([shift] * PICKED_BLOCKS, 1))
            fade = jnp.exp2(-top)
            out, total = summed(weight.astype(jnp.bfloat16), value)
            out = out + acc_ref[i, part, :].astype(jnp.float32) * fade
            result = (out / (total + fade)).astype(out_ref.dtype)
            for g in range(PICK_ROWS // BLOCK_TOKENS):
                at = slice(g * BLOCK_TOKENS, (g + 1) * BLOCK_TOKENS)
                out_ref[i, :, first + g * HEAD_SIZE : first + (g + 1) * HEAD_SIZE] = result[at]

    sums_load(0).start()
    for j in range(PICK_AHEAD):
        start_round(0, j)
    for b in range(1, BLOCKS):
        sums_load(b).start()

    for b in range(BLOCKS):
        sums_load(b).wait()

        @pl.loop(0, rounds)
        def _(j):
            @pl.when(j + PICK_AHEAD < rounds)
            def _():
                start_round(b, j + PICK_AHEAD)

            if b + 1 < BLOCKS:

                @pl.when(j + PICK_AHEAD >= rounds)
                def _():
                    start_round(b + 1, j + PICK_AHEAD - rounds)

            for u in range(PICK_UNROLL):
                for copy in loads(b, j * PICK_UNROLL + u):
                    copy.wait()

            for u in range(PICK_UNROLL):
                h = j * PICK_UNROLL + u
                step(b, h)
                store(b, h).start()

    for b in range(BLOCKS):
        for h in range(KEY_VALUE_HEADS):
            store(b, h).wait()


def shards(queries, keys, values, positions, picks):
    tokens = queries.shape[0]
    window = lax.axis_size("ctx")
    limit = max(1, BLOCKS * KEY_VALUE_HEADS * PICKED_BLOCKS // window)
    me = lax.axis_index("ctx").astype(jnp.int32).reshape(1)
    bf16 = jnp.bfloat16
    vmem = pl.BlockSpec(memory_space=pltpu.MemorySpace.VMEM)
    smem = pl.BlockSpec(memory_space=SMEM)
    hbm = pl.BlockSpec(memory_space=pl.ANY)

    behind = [((i - 1) % window, i) for i in range(window)]
    near_v = lax.ppermute(values, "ctx", behind)
    rotated_keys, last, cosine, sine, table, slot = pl.pallas_call(
        functools.partial(prep_kernel, limit),
        out_shape=(
            jax.ShapeDtypeStruct((tokens, KEY_WIDTH), bf16),
            jax.ShapeDtypeStruct((BLOCK_TOKENS, 2 * KEY_WIDTH), bf16),
            jax.ShapeDtypeStruct((tokens, HEAD_SIZE), jnp.float32),
            jax.ShapeDtypeStruct((tokens, HEAD_SIZE), jnp.float32),
            jax.ShapeDtypeStruct((window, 1, limit), jnp.int32),
            jax.ShapeDtypeStruct((BLOCKS * KEY_VALUE_HEADS, PICKED_BLOCKS), jnp.int32),
        ),
        in_specs=[smem, vmem, hbm, vmem, vmem],
        out_specs=(vmem, vmem, vmem, vmem, smem, smem),
        scratch_shapes=[pltpu.SMEM((window,), jnp.int32), pltpu.SemaphoreType.DMA],
        name="prep",
    )(picks.transpose(0, 2, 1), keys, values, positions.reshape(BLOCKS, BLOCK_TOKENS), jnp.asarray(frequencies()))

    near_k = lax.ppermute(rotated_keys, "ctx", behind)
    wanted = lax.all_to_all(table, "ctx", split_axis=0, concat_axis=0, tiled=True)
    wanted, near_k, near_v = lax.optimization_barrier((wanted, near_k, near_v))
    far_even = lax.ppermute(last, "ctx", [((i - 2) % window, i) for i in range(0, window, 2)])

    answer = pl.pallas_call(
        gather_kernel,
        out_shape=jax.ShapeDtypeStruct((window, limit, 2, BLOCK_TOKENS, HEAD_SIZE), bf16),
        in_specs=[smem, vmem, vmem],
        out_specs=hbm,
        scratch_shapes=[pltpu.SemaphoreType.DMA((2, window, limit))],
        cost_estimate=pl.CostEstimate(flops=0, bytes_accessed=60 << 20, transcendentals=0),
        name="gather",
    )(wanted, rotated_keys, values)
    landed = lax.all_to_all(answer, "ctx", split_axis=0, concat_axis=0, tiled=True)
    landed = landed.reshape(window * limit, 2, BLOCK_TOKENS, HEAD_SIZE)

    band_flops = 4 * BLOCKS * QUERY_HEADS * BLOCK_TOKENS * LOCAL_BAND_SIZE * BLOCK_TOKENS * HEAD_SIZE
    full = (KEY_VALUE_HEADS, ROWS, HEAD_SIZE)

    def band(b, weight, *far):
        return pl.pallas_call(
            functools.partial(band_kernel, b),
            out_shape=(
                jax.ShapeDtypeStruct(full, bf16),
                jax.ShapeDtypeStruct(full, bf16),
                jax.ShapeDtypeStruct((ROWS, HEAD_SIZE), bf16),
            ),
            in_specs=[smem] + [vmem] * (7 + len(far)),
            out_specs=(vmem,) * 3,
            cost_estimate=pl.CostEstimate(flops=weight * band_flops, bytes_accessed=8 << 20, transcendentals=1 << 22),
            compiler_params=pltpu.CompilerParams(vmem_limit_bytes=30 << 20),
            name="band",
        )(me, queries, cosine, sine, near_k, near_v, rotated_keys, values, *far)

    second = band(1, 50)
    edge_k, edge_v, _ = lax.optimization_barrier((near_k, near_v, second[2]))
    edge = jnp.concatenate([edge_k[tokens - BLOCK_TOKENS :], edge_v[tokens - BLOCK_TOKENS :]], 1)
    far_odd = lax.ppermute(edge, "ctx", [(i ^ 1, i) for i in range(window)])
    first = band(0, 1, far_even, far_odd)

    count = BLOCKS * KEY_VALUE_HEADS
    narrow = (count, ROWS, HEAD_SIZE)
    return pl.pallas_call(
        picks_kernel,
        out_shape=jax.ShapeDtypeStruct((tokens, QUERY_HEADS * HEAD_SIZE), bf16),
        in_specs=[smem] + [hbm] * (1 + 3 * BLOCKS),
        out_specs=hbm,
        scratch_shapes=[
            pltpu.VMEM(narrow, bf16),
            pltpu.VMEM((count, PICKED_BLOCKS, 2, BLOCK_TOKENS, HEAD_SIZE), bf16),
            pltpu.VMEM(narrow, bf16),
            pltpu.VMEM((BLOCKS, ROWS, HEAD_SIZE), bf16),
            pltpu.VMEM((count, BLOCK_TOKENS, ROWS), bf16),
            pltpu.SemaphoreType.DMA((count, PICKED_BLOCKS + 2)),
            pltpu.SemaphoreType.DMA((count,)),
            pltpu.SemaphoreType.DMA((BLOCKS,)),
        ],
        cost_estimate=pl.CostEstimate(flops=2 * band_flops, bytes_accessed=16 << 20, transcendentals=1 << 22),
        compiler_params=pltpu.CompilerParams(vmem_limit_bytes=58 << 20),
        name="picks",
    )(slot, landed, *first, *second)


def solution(mesh):
    return jax.shard_map(
        shards,
        mesh=mesh,
        in_specs=(
            P(("groups", "ctx"), None),
            P(("groups", "ctx"), None),
            P(("groups", "ctx"), None),
            P(("groups", "ctx")),
            P(("groups", "ctx"), None, None),
        ),
        out_specs=P(("groups", "ctx"), None),
        check_vma=False,
    )
```
